128 devices in a mesh: sx: 4 (over y), ly: 32 (over z, x, core).
Axes of the slice: x: 4, y: 4, z: 4, core: 2. Of those that a mesh axis runs over, the one named last changes fastest.
Arguments:
- tensor: float32 [1024, 1280, 512], P('sx', 'ly'), may hold values from -6 to 6
- factor_y: float32 [512, 160], replicated, may hold values from -6 to 6
- factor_z: float32 [1280, 160], P('ly'), may hold values from -6 to 6
- test_matrix: float32 [1280, 160], replicated, may hold values from -6 to 6
Outputs:
- basis_first: float32 [1024, 160], P('sx')
- basis_second: float32 [160, 512, 160], P('sx', 'ly')
- last_core: float32 [160, 1280], replicated
The draws below stay inside these ranges and needn't reach their ends.
All inputs are finite; a program needn't handle non-finite values.
Results may differ from the reference program's by a relative error of at most 0.0003.
Values sent between devices are 32-bit elements; how exact they have to be, the bound alone decides.
No kernel may reach another device: no remote copies, remote signals or barrier semaphores. Data moves between devices by JAX's collectives and lax.ppermute only.
A program may use at most 192 MiB of HBM per device.

```python
import math
import jax
import jax.numpy as jnp
from jax import lax

Y = 512
R = 160
R2 = 160
X = 1024
Z = 1280


def draw_tensor(key, part):
    mode_count = 2 * R + 128
    subkeys = jax.random.split(key, 3)
    half_width = math.sqrt(3.0)
    along_x = jax.random.uniform(subkeys[0], (X, mode_count), jnp.float32, -half_width, half_width)
    along_z = jax.random.uniform(subkeys[1], (Z, mode_count), jnp.float32, -half_width, half_width)
    along_y = jax.random.uniform(subkeys[2], (Y, mode_count), jnp.float32, -half_width, half_width)
    amplitude = 1.0
    decay_ratio = 10.0 ** (-1.0 / 72.0)
    norm_total = math.sqrt((1.0 - decay_ratio ** (2 * mode_count)) / (1.0 - decay_ratio ** 2))
    orders = jnp.arange(mode_count, dtype=jnp.float32)
    weights = amplitude / norm_total * jnp.power(jnp.float32(decay_ratio), orders)
    scaled_x = along_x * weights[None, :]
    block_rows = math.gcd(X, 32)
    grouped = scaled_x.reshape(X // block_rows, block_rows, mode_count)

    def fill_rows(x_rows):
        paired = x_rows[:, None, :] * along_z[None, :, :]
        products = jnp.dot(paired.reshape(block_rows * Z, mode_count), along_y.T, precision=lax.Precision.HIGHEST)
        return products.reshape(block_rows, Z, Y)
    slab_value = lax.map(fill_rows, grouped).reshape(X, Z, Y)
    return jnp.clip(slab_value, -6.0, 6.0)


def levels(rng, dims, shards, smallest, top_value):
    def one(axis_at, shards_of):
        draws = jax.random.uniform(jax.random.fold_in(jax.random.fold_in(rng, 6), axis_at), (shards_of,), jnp.float32, smallest / len(shards), top_value / len(shards))
        return jnp.repeat(jnp.exp(draws), dims[axis_at] // shards_of).reshape((-1,) + (1,) * (len(dims) - axis_at - 1))

    loudness = one(*shards[0])
    for cut in shards[1:]:
        loudness = loudness * one(*cut)
    return loudness


def centred(stream_key, dims, deviation, bound, shards=(), kind=jnp.bfloat16):
    entries = jax.random.normal(stream_key, dims, jnp.float32) * deviation
    if len(shards) > 0:
        entries = levels(stream_key, dims, shards, -0.22, 0.18) * entries
    return jnp.clip(entries, min=-bound, max=bound).astype(kind)


def setup_inputs(seed: int = 0) -> dict:
    seeds = jax.random.split(jax.random.key(seed), 5)
    return {
        "tensor": draw_tensor(jax.random.fold_in(seeds[4], 71), 0),
        "factor_y": centred(seeds[1], (Y, R), 1.0, 6.0, (), jnp.float32),
        "factor_z": centred(seeds[2], (Z, R), 1.0, 6.0, ((0, 32),), jnp.float32),
        "test_matrix": centred(seeds[3], (Z, R2), 1.0, 6.0, (), jnp.float32),
    }


def orthonormalize(matrix):
    gram = jnp.dot(matrix.T, matrix, precision=lax.Precision.HIGHEST)
    lower = jnp.linalg.cholesky(gram)
    ident = jnp.eye(gram.shape[0], dtype=gram.dtype)
    inverse = jax.scipy.linalg.solve_triangular(lower, ident, lower=True)
    return jnp.dot(matrix, inverse.T, precision=lax.Precision.HIGHEST)

def reference(tensor, factor_y, factor_z, test_matrix):
    partial_value = jnp.dot(tensor.reshape(X * Z, Y), factor_y, precision=lax.Precision.HIGHEST).reshape(X, Z, R)
    sketch = lax.optimization_barrier(jnp.sum(partial_value * factor_z[None], axis=1))
    q_first = orthonormalize(orthonormalize(sketch))
    core = jnp.dot(q_first.T, tensor.reshape(X, Z * Y), precision=lax.Precision.HIGHEST).reshape(R, Z, Y)
    second = jnp.einsum('rzy,zk->ryk', core, test_matrix, precision=lax.Precision.HIGHEST)
    q_second = orthonormalize(orthonormalize(second.reshape(R * Y, R2))).reshape(R, Y, R2)
    last_core = jnp.einsum('rzy,ryk->kz', core, q_second, precision=lax.Precision.HIGHEST)
    core_scale = math.sqrt(R2 / (X * Y))
    return (math.sqrt(X) * q_first, math.sqrt(R * Y) * q_second, core_scale * last_core)
```

```python
import math

import jax
import jax.numpy as jnp
from jax import lax
from jax.experimental import pallas as pl
from jax.experimental.pallas import tpu as pltpu
from jax.sharding import PartitionSpec as P

HI = lax.Precision.HIGHEST
F32 = jnp.float32
VMEM_LIMIT = 56 * 1024 * 1024


def mm(a, b):
    return lax.dot_general(a, b, (((1,), (0,)), ((), ())), precision=HI, preferred_element_type=F32)


def mm_nt(a, b):
    return lax.dot_general(a, b, (((1,), (1,)), ((), ())), precision=HI, preferred_element_type=F32)


def inverse_factor(tiles, size):
    count = size // 8
    lanes = -(-size // 128)
    lane = lax.broadcasted_iota(jnp.int32, (8, 128), 1)
    sub = lax.broadcasted_iota(jnp.int32, (8, 128), 0)
    work = [list(row) for row in tiles]
    diag = [None] * count
    for j in range(size):
        t0, s0 = divmod(j, 8)
        l0, c0 = divmod(j, 128)
        cols = [
            jnp.broadcast_to(work[t][l0][:, c0 : c0 + 1], (8, 128)) for t in range(t0, count)
        ]
        pivot = jnp.broadcast_to(cols[0][s0 : s0 + 1, :], (8, 128))
        inv = 1.0 / pivot
        rows = [jnp.broadcast_to(work[t0][l][s0 : s0 + 1, :], (8, 128)) for l in range(lanes)]
        here = sub == s0
        diag[t0] = cols[0] if s0 == 0 else jnp.where(here, cols[0], diag[t0])
        for t in range(t0, count):
            if t == t0 and s0 == 7:
                continue
            factor = cols[t - t0] * inv
            if t == t0:
                factor = jnp.where(sub > s0, factor, 0.0)
            for l in range(lanes):
                new = work[t][l] - factor * rows[l]
                if l == l0:
                    col_new = -factor
                    if t == t0:
                        new = jnp.where((lane == c0) & (sub > s0), col_new, new)
                    else:
                        new = jnp.where(lane == c0, col_new, new)
                work[t][l] = new
    out = []
    for t in range(count):
        scale = lax.rsqrt(diag[t])
        scale = scale * (1.5 - 0.5 * diag[t] * scale * scale)
        row = []
        for l in range(lanes):
            pos = lane + 128 * l
            idx = sub + 8 * t
            val = jnp.where(pos == idx, 1.0, jnp.where(pos < idx, work[t][l], 0.0))
            row.append(val * scale)
        out.append(row)
    return out


def put_inverse(tiles, size, out_ref):
    inverse = inverse_factor(tiles, size)
    for t, row in enumerate(inverse):
        for l, val in enumerate(row):
            out_ref[8 * t : 8 * t + 8, 128 * l : 128 * l + 128] = val


def tiles_of(ref, size, row0=0):
    lanes = -(-size // 128)
    return [
        [ref[row0 + 8 * t : row0 + 8 * t + 8, 128 * l : 128 * l + 128] for l in range(lanes)]
        for t in range(size // 8)
    ]


def first_kernel(index_ref, sketch_ref, q_ref, basis_ref, gram_ref, inv_ref, qt_ref, *, rank, rows_x, scale):
    sk = sketch_ref[...]
    gram_ref[...] = jnp.zeros_like(gram_ref)
    gram_ref[:, :rank] = lax.dot_general(
        sk, sk, (((0,), (0,)), ((), ())), precision=HI, preferred_element_type=F32
    )
    put_inverse(tiles_of(gram_ref, rank), rank, inv_ref)
    qt = mm_nt(inv_ref[:, :rank], sk)
    qt_ref[...] = qt
    gram_ref[:, :rank] = mm_nt(qt, qt)
    put_inverse(tiles_of(gram_ref, rank), rank, inv_ref)
    at = pl.multiple_of(index_ref[0] * rows_x, 128)
    mine = mm(inv_ref[:, :rank], qt_ref[:, pl.ds(at, rows_x)])
    q_ref[...] = mine
    basis_ref[...] = scale * mine


def first_basis(sketch, index, rows_x, scale):
    total, rank = sketch.shape
    wide = -(-rank // 128) * 128
    shape = jax.ShapeDtypeStruct((rank, rows_x), F32)
    import functools

    vmem = pl.BlockSpec(memory_space=pltpu.VMEM)
    return pl.pallas_call(
        functools.partial(first_kernel, rank=rank, rows_x=rows_x, scale=scale),
        out_shape=(shape, shape),
        in_specs=[pl.BlockSpec(memory_space=pltpu.SMEM), vmem],
        out_specs=(vmem, vmem),
        scratch_shapes=[
            pltpu.VMEM((rank, wide), F32),
            pltpu.VMEM((rank, wide), F32),
            pltpu.VMEM((rank, total), F32),
        ],
        compiler_params=pltpu.CompilerParams(vmem_limit_bytes=VMEM_LIMIT),
        name="first_basis",
    )(index, sketch)


def product_kernel(qt_ref, slab_ref, out_ref, *, cols_z, rows_x, parts, rank_part):
    qt = qt_ref[...]

    def body(step, carry):
        z = step * 2
        left = slab_ref[pl.ds(z, rows_x, stride=cols_z), :]
        right = slab_ref[pl.ds(z + 1, rows_x, stride=cols_z), :]
        both = mm(qt, jnp.concatenate([left, right], axis=1))
        for s in range(parts):
            piece = both[s * rank_part : (s + 1) * rank_part]
            out_ref[s, 0, pl.ds(z, rank_part, stride=cols_z), :] = piece[:, :128]
            out_ref[s, 0, pl.ds(z + 1, rank_part, stride=cols_z), :] = piece[:, 128:]
        return carry

    lax.fori_loop(0, cols_z // 2, body, 0)


def product(qt, tensor, parts):
    import functools

    rows_x, cols_z, cols_y = tensor.shape
    rank = qt.shape[0]
    blocks = cols_y // 128
    rank_part = rank // parts
    flat = tensor.reshape(rows_x * cols_z, cols_y)
    return pl.pallas_call(
        functools.partial(
            product_kernel, cols_z=cols_z, rows_x=rows_x, parts=parts, rank_part=rank_part
        ),
        grid=(blocks,),
        out_shape=jax.ShapeDtypeStruct((parts, blocks, rank_part * cols_z, 128), F32),
        in_specs=[
            pl.BlockSpec((rank, rows_x), lambda i: (0, 0)),
            pl.BlockSpec((rows_x * cols_z, 128), lambda i: (0, i)),
        ],
        out_specs=pl.BlockSpec((parts, 1, rank_part * cols_z, 128), lambda i: (0, i, 0, 0)),
        compiler_params=pltpu.CompilerParams(vmem_limit_bytes=VMEM_LIMIT),
        name="product",
    )(qt, flat)


def second_kernel(recv_ref, test_ref, core_ref, second_ref, gram_out_ref, gram_ref, *, width):
    step = pl.program_id(0)
    core = recv_ref[0, :, 0] + recv_ref[1, :, 0]
    core = core + (recv_ref[2, :, 0] + recv_ref[3, :, 0])
    core = core.reshape(core_ref.shape[1:])
    core_ref[0] = core
    sec = mm(test_ref[...], core)
    second_ref[0] = sec
    part = mm_nt(sec, sec)

    @pl.when(step == 0)
    def _():
        gram_ref[:, :width] = part

    @pl.when(step > 0)
    def _():
        gram_ref[:, :width] = gram_ref[:, :width] + part

    @pl.when(step == pl.num_programs(0) - 1)
    def _():
        gram_out_ref[...] = jnp.zeros_like(gram_out_ref)
        gram_out_ref[:width, :] = gram_ref[:, :128]
        gram_out_ref[width : 2 * width, : width - 128] = gram_ref[:, 128:width]


def second_stage(recv, test_t, devices):
    import functools

    parts, groups, ranks, cols_z, lanes = recv.shape
    width, total_z = test_t.shape
    gram_rows = 4 * devices
    return pl.pallas_call(
        functools.partial(second_kernel, width=width),
        grid=(ranks,),
        out_shape=(
            jax.ShapeDtypeStruct((ranks, total_z, lanes), F32),
            jax.ShapeDtypeStruct((ranks, width, lanes), F32),
            jax.ShapeDtypeStruct((gram_rows, 128), F32),
        ),
        in_specs=[
            pl.BlockSpec((parts, groups, 1, cols_z, lanes), lambda i: (0, 0, i, 0, 0)),
            pl.BlockSpec((width, total_z), lambda i: (0, 0)),
        ],
        out_specs=(
            pl.BlockSpec((1, total_z, lanes), lambda i: (i, 0, 0)),
            pl.BlockSpec((1, width, lanes), lambda i: (i, 0, 0)),
            pl.BlockSpec((gram_rows, 128), lambda i: (0, 0)),
        ),
        scratch_shapes=[pltpu.VMEM((width, -(-width // 128) * 128), F32)],
        compiler_params=pltpu.CompilerParams(vmem_limit_bytes=VMEM_LIMIT),
        name="second_stage",
    )(recv, test_t)


def middle_kernel(gram_ref, second_ref, core_ref, q_ref, sums_ref, inv_ref, wide_ref, *, width):
    tiles = [
        [gram_ref[8 * t : 8 * t + 8, :], gram_ref[width + 8 * t : width + 8 * t + 8, :]]
        for t in range(width // 8)
    ]
    put_inverse(tiles, width, inv_ref)
    inv = inv_ref[:, :width]
    total_z = core_ref.shape[1]
    gram = None
    last = None
    for r in range(second_ref.shape[0]):
        q = mm(inv, second_ref[r])
        q_ref[r] = q
        g = mm_nt(q, q)
        h = mm_nt(q, core_ref[r])
        gram = g if gram is None else gram + g
        last = h if last is None else last + h
    wide_ref[:, total_z:] = jnp.zeros((width, wide_ref.shape[1] - total_z), F32)
    wide_ref[:, :total_z] = last
    wide_ref[:, total_z : total_z + width] = gram
    lanes = wide_ref.shape[1] // 128
    for t in range(width // 8):
        for l in range(lanes):
            sums_ref[t * lanes + l] = wide_ref[8 * t : 8 * t + 8, 128 * l : 128 * l + 128]
    for n in range(width // 8 * lanes, sums_ref.shape[0]):
        sums_ref[n] = jnp.zeros((8, 128), F32)


def middle_stage(gram, second, core, devices):
    import functools

    ranks, width, lanes = second.shape
    total_z = core.shape[1]
    wide = total_z + -(-width // 128) * 128
    count = width // 8 * (wide // 128)
    count = -(-count // devices) * devices
    vmem = pl.BlockSpec(memory_space=pltpu.VMEM)
    return pl.pallas_call(
        functools.partial(middle_kernel, width=width),
        out_shape=(
            jax.ShapeDtypeStruct((ranks, width, lanes), F32),
            jax.ShapeDtypeStruct((count, 8, 128), F32),
        ),
        in_specs=[vmem, vmem, vmem],
        out_specs=(vmem, vmem),
        scratch_shapes=[
            pltpu.VMEM((width, -(-width // 128) * 128), F32),
            pltpu.VMEM((width, wide), F32),
        ],
        compiler_params=pltpu.CompilerParams(vmem_limit_bytes=VMEM_LIMIT),
        name="middle_stage",
    )(gram, second, core)


def last_kernel(sums_ref, q_ref, basis_ref, last_ref, inv_ref, wide_ref, *, width, lanes, scales):
    first = last_ref.shape[1] // 128
    tiles = [
        [sums_ref[t * lanes + first + l] for l in range(lanes - first)] for t in range(width // 8)
    ]
    put_inverse(tiles, width, inv_ref)
    inv = inv_ref[:, :width]
    for t in range(width // 8):
        for l in range(first):
            wide_ref[8 * t : 8 * t + 8, 128 * l : 128 * l + 128] = sums_ref[t * lanes + l]
    last_ref[...] = scales[1] * mm(inv, wide_ref[...])
    for r in range(q_ref.shape[0]):
        basis = scales[0] * mm(inv, q_ref[r])
        basis = basis.T
        for m in range(basis_ref.shape[0]):
            rows = basis_ref.shape[2]
            basis_ref[m, r] = basis[m * rows : (m + 1) * rows, :]


def last_stage(sums, q, total_z, members, scales):
    import functools

    ranks, width, span = q.shape
    lanes = (total_z + -(-width // 128) * 128) // 128
    vmem = pl.BlockSpec(memory_space=pltpu.VMEM)
    return pl.pallas_call(
        functools.partial(last_kernel, width=width, lanes=lanes, scales=scales),
        out_shape=(
            jax.ShapeDtypeStruct((members, ranks, span // members, width), F32),
            jax.ShapeDtypeStruct((width, total_z), F32),
        ),
        in_specs=[vmem, vmem],
        out_specs=(vmem, vmem),
        scratch_shapes=[
            pltpu.VMEM((width, -(-width // 128) * 128), F32),
            pltpu.VMEM((width, total_z), F32),
        ],
        compiler_params=pltpu.CompilerParams(vmem_limit_bytes=VMEM_LIMIT),
        name="last_stage",
    )(sums, q)


def swap(pieces, axes, groups=None):
    return lax.all_to_all(pieces, axes, 0, 0, axis_index_groups=groups, tiled=True)


def share(piece, axes, count):
    return swap(jnp.broadcast_to(piece[None], (count,) + piece.shape), axes)


def shards(tensor, factor_y, factor_z, test_matrix):
    rows_x, cols_z, cols_y = tensor.shape
    rank = factor_y.shape[1]
    width = test_matrix.shape[1]
    n_sx = lax.axis_size("sx")
    n_ly = lax.axis_size("ly")
    both = ("sx", "ly")
    devices = n_sx * n_ly
    total_x = rows_x * n_sx
    total_z = cols_z * n_ly
    partial_value = jnp.dot(tensor.reshape(rows_x * cols_z, cols_y), factor_y, precision=HI)
    partial_value = partial_value.reshape(rows_x, cols_z, rank)
    local_sketch = jnp.sum(partial_value * factor_z[None], axis=1)
    mine = jnp.sum(swap(local_sketch.reshape(n_ly, rows_x // n_ly, rank), "ly"), axis=0)
    sketch = share(mine, both, devices).reshape(total_x, rank)
    index = lax.axis_index("sx").astype(jnp.int32).reshape(1)
    qt, basis_t = first_basis(sketch, index, rows_x, math.sqrt(total_x))

    blocks = cols_y // 128
    members = n_ly // blocks
    ranks = rank // (n_sx * members)
    partial_core = product(qt, tensor, n_sx)
    recv = swap(partial_core.reshape(devices, ranks, cols_z, 128), both)
    recv = recv.reshape(n_sx, n_ly, ranks, cols_z, 128)
    core, second, gram = second_stage(recv, test_matrix.T, devices)
    gram = jnp.sum(swap(gram.reshape(devices, 4, 128), both), axis=0)
    gram = share(gram, both, devices).reshape(devices * 4, 128)
    q_one, sums = middle_stage(gram, second, core, devices)
    per = sums.shape[0] // devices
    sums = jnp.sum(swap(sums.reshape(devices, per, 8, 128), both), axis=0)
    sums = share(sums, both, devices).reshape(devices * per, 8, 128)
    scales = (math.sqrt(rank * cols_y), math.sqrt(width / (total_x * cols_y)))
    basis, last_core = last_stage(sums, q_one, total_z, members, scales)
    groups = [[b * members + m for m in range(members)] for b in range(blocks)]
    basis = swap(basis, "ly", groups)
    basis_second = basis.reshape(members * ranks, 128 // members, width)
    return (basis_t.T, basis_second, last_core)


def solution(mesh):
    return jax.shard_map(
        shards,
        mesh=mesh,
        in_specs=(P("sx", "ly", None), P(), P("ly", None), P()),
        out_specs=(P("sx", None), P("sx", "ly", None), P()),
        check_vma=False,
    )
```

```python
import math

import jax
import jax.numpy as jnp
from jax import lax
from jax.experimental import pallas as pl
from jax.experimental.pallas import tpu as pltpu
from jax.sharding import PartitionSpec as P

HI = lax.Precision.HIGHEST
F32 = jnp.float32
VMEM_LIMIT = 56 * 1024 * 1024


def mm(a, b):
    return lax.dot_general(a, b, (((1,), (0,)), ((), ())), precision=HI, preferred_element_type=F32)


def mm_nt(a, b):
    return lax.dot_general(a, b, (((1,), (1,)), ((), ())), precision=HI, preferred_element_type=F32)


GROUP = 5


def tiles_of(ref, size, row0=0):
    lanes = -(-size // 128)
    return [
        [ref[row0 + 8 * t : row0 + 8 * t + 8, 128 * l : 128 * l + 128] for l in range(lanes)]
        for t in range(size // 8)
    ]

def spread(row, tile):
    return jnp.broadcast_to(tile[row : row + 1, :], (8, 128))

def put_inverse(tiles, size, out_ref, group=GROUP):
    count = size // 8
    lanes = -(-size // 128)
    lane = lax.broadcasted_iota(jnp.int32, (8, 128), 1)
    sub = lax.broadcasted_iota(jnp.int32, (8, 128), 0)
    work = [list(r) for r in tiles]
    for g in range(0, count, group):
        end = min(g + group, count)
        done = []
        for p in range(g, end):
            l0, c0 = divmod(8 * p, 128)
            span = range(p, end)
            cols = {t: [jnp.broadcast_to(work[t][l0][:, c0 + i : c0 + i + 1], (8, 128)) for i in range(8)] for t in span}
            block = list(cols[p])
            unit = [jnp.where(sub == c, 1.0, 0.0) for c in range(8)]
            diag = None
            for i in range(8):
                diag = block[i] if i == 0 else jnp.where(sub == i, block[i], diag)
                if i == 7:
                    break
                factor = block[i] * spread(i, 1.0 / block[i])
                factor = jnp.where(sub > i, factor, 0.0)
                for m in range(i + 1, 8):
                    block[m] = block[m] - factor * spread(i, block[m])
                for c in range(i + 1):
                    unit[c] = unit[c] - factor * spread(i, unit[c])
            root = lax.rsqrt(diag)
            root = root * (1.5 - 0.5 * diag * root * root)
            inv = [u * root for u in unit]
            src = list(work[p])
            inside = (lane >= c0) & (lane < c0 + 8)
            src[l0] = jnp.where(inside, jnp.where(lane - c0 == sub, 1.0, 0.0), src[l0])
            rows = []
            for l in range(lanes):
                terms = [inv[i] * spread(i, src[l]) for i in range(8)]
                rows.append(((terms[0] + terms[1]) + (terms[2] + terms[3])) + ((terms[4] + terms[5]) + (terms[6] + terms[7])))
            for l in range(lanes):
                pos = lane + 128 * l
                out_ref[8 * p : 8 * p + 8, 128 * l : 128 * l + 128] = jnp.where(pos <= sub + 8 * p, rows[l], 0.0)
            done.append(rows)
            for t in range(p + 1, end):
                factors = []
                for m in range(8):
                    terms = [cols[t][i] * spread(m, inv[i]) for i in range(m + 1)]
                    while len(terms) > 1:
                        terms = [a + b for a, b in zip(terms[::2], terms[1::2])] + ([terms[-1]] if len(terms) % 2 else [])
                    factors.append(terms[0])
                for l in range(lanes):
                    old = work[t][l]
                    if l == l0:
                        old = jnp.where(inside, 0.0, old)
                    terms = [factors[m] * spread(m, rows[l]) for m in range(8)]
                    work[t][l] = old - (((terms[0] + terms[1]) + (terms[2] + terms[3])) + ((terms[4] + terms[5]) + (terms[6] + terms[7])))
        if end < count:
            left = jnp.concatenate([jnp.concatenate(r, axis=1) for r in done], axis=0)
            pos = lax.broadcasted_iota(jnp.int32, left.shape, 1)
            own = lax.broadcasted_iota(jnp.int32, left.shape, 0) + 8 * g
            right = jnp.where((pos > own) & (pos < 8 * end), 0.0, left)
            outer = lax.dot_general(left, right, (((0,), (0,)), ((), ())), precision=HI, preferred_element_type=F32)
            for t in range(end, count):
                for l in range(lanes):
                    pos = lane + 128 * l
                    old = work[t][l]
                    if 128 * l < 8 * end and 128 * l + 128 > 8 * g:
                        old = jnp.where((pos >= 8 * g) & (pos < 8 * end), 0.0, old)
                    work[t][l] = old - outer[8 * t : 8 * t + 8, 128 * l : 128 * l + 128]


def first_kernel(index_ref, sketch_ref, q_ref, basis_ref, gram_ref, inv_ref, qt_ref, *, rank, rows_x, scale):
    sk = sketch_ref[...]
    gram_ref[...] = jnp.zeros_like(gram_ref)
    gram_ref[:, :rank] = lax.dot_general(
        sk, sk, (((0,), (0,)), ((), ())), precision=HI, preferred_element_type=F32
    )
    put_inverse(tiles_of(gram_ref, rank), rank, inv_ref)
    qt = mm_nt(inv_ref[:, :rank], sk)
    qt_ref[...] = qt
    gram_ref[:, :rank] = mm_nt(qt, qt)
    put_inverse(tiles_of(gram_ref, rank), rank, inv_ref)
    at = pl.multiple_of(index_ref[0] * rows_x, 128)
    mine = mm(inv_ref[:, :rank], qt_ref[:, pl.ds(at, rows_x)])
    q_ref[...] = mine
    basis_ref[...] = scale * mine


def first_basis(sketch, index, rows_x, scale):
    total, rank = sketch.shape
    wide = -(-rank // 128) * 128
    shape = jax.ShapeDtypeStruct((rank, rows_x), F32)
    import functools

    vmem = pl.BlockSpec(memory_space=pltpu.VMEM)
    return pl.pallas_call(
        functools.partial(first_kernel, rank=rank, rows_x=rows_x, scale=scale),
        out_shape=(shape, shape),
        in_specs=[pl.BlockSpec(memory_space=pltpu.SMEM), vmem],
        out_specs=(vmem, vmem),
        scratch_shapes=[
            pltpu.VMEM((rank, wide), F32),
            pltpu.VMEM((rank, wide), F32),
            pltpu.VMEM((rank, total), F32),
        ],
        compiler_params=pltpu.CompilerParams(vmem_limit_bytes=VMEM_LIMIT),
        name="first_basis",
    )(index, sketch)


def split(value):
    high = value.astype(jnp.bfloat16)
    rest = value - high.astype(F32)
    middle = rest.astype(jnp.bfloat16)
    low = (rest - middle.astype(F32)).astype(jnp.bfloat16)
    return high, middle, low


def dot_bf16(a, b):
    return lax.dot_general(a, b, (((1,), (0,)), ((), ())), preferred_element_type=F32)


def product_kernel(qt_ref, slab_ref, out_ref, left_ref, *, cols_z, rows_x, parts, rank_part):
    rank = parts * rank_part

    @pl.when(pl.program_id(0) == 0)
    def _():
        for n, piece in enumerate(split(qt_ref[...])):
            left_ref[n * rank : (n + 1) * rank, :] = piece

    def body(step, carry):
        z = step * 2
        left = slab_ref[pl.ds(z, rows_x, stride=cols_z), :]
        right = slab_ref[pl.ds(z + 1, rows_x, stride=cols_z), :]
        high, middle, low = split(jnp.concatenate([left, right], axis=1))
        first = dot_bf16(left_ref[...], high)
        second = dot_bf16(left_ref[: 2 * rank, :], middle)
        third = dot_bf16(left_ref[:rank, :], low)
        both = first[:rank] + (
            (first[rank : 2 * rank] + second[:rank]) + (first[2 * rank :] + (second[rank:] + third))
        )
        for s in range(parts):
            piece = both[s * rank_part : (s + 1) * rank_part]
            out_ref[s, 0, pl.ds(z, rank_part, stride=cols_z), :] = piece[:, :128]
            out_ref[s, 0, pl.ds(z + 1, rank_part, stride=cols_z), :] = piece[:, 128:]
        return carry

    lax.fori_loop(0, cols_z // 2, body, 0, unroll=10)


def product(qt, tensor, parts):
    import functools

    rows_x, cols_z, cols_y = tensor.shape
    rank = qt.shape[0]
    blocks = cols_y // 128
    rank_part = rank // parts
    flat = tensor.reshape(rows_x * cols_z, cols_y)
    return pl.pallas_call(
        functools.partial(
            product_kernel, cols_z=cols_z, rows_x=rows_x, parts=parts, rank_part=rank_part
        ),
        grid=(blocks,),
        out_shape=jax.ShapeDtypeStruct((parts, blocks, rank_part * cols_z, 128), F32),
        in_specs=[
            pl.BlockSpec((rank, rows_x), lambda i: (0, 0)),
            pl.BlockSpec((rows_x * cols_z, 128), lambda i: (0, i)),
        ],
        out_specs=pl.BlockSpec((parts, 1, rank_part * cols_z, 128), lambda i: (0, i, 0, 0)),
        scratch_shapes=[pltpu.VMEM((3 * rank, rows_x), jnp.bfloat16)],
        compiler_params=pltpu.CompilerParams(vmem_limit_bytes=VMEM_LIMIT),
        name="product",
    )(qt, flat)


def second_kernel(recv_ref, test_ref, core_ref, second_ref, gram_out_ref, gram_ref, *, width):
    step = pl.program_id(0)
    core = recv_ref[0, :, 0] + recv_ref[1, :, 0]
    core = core + (recv_ref[2, :, 0] + recv_ref[3, :, 0])
    core = core.reshape(core_ref.shape[1:])
    core_ref[0] = core
    sec = mm(test_ref[...], core)
    second_ref[0] = sec
    part = mm_nt(sec, sec)

    @pl.when(step == 0)
    def _():
        gram_ref[:, :width] = part

    @pl.when(step > 0)
    def _():
        gram_ref[:, :width] = gram_ref[:, :width] + part

    @pl.when(step == pl.num_programs(0) - 1)
    def _():
        gram_out_ref[...] = jnp.zeros_like(gram_out_ref)
        gram_out_ref[:width, :] = gram_ref[:, :128]
        gram_out_ref[width : 2 * width, : width - 128] = gram_ref[:, 128:width]


def second_stage(recv, test_t, devices):
    import functools

    parts, groups, ranks, cols_z, lanes = recv.shape
    width, total_z = test_t.shape
    gram_rows = 4 * devices
    return pl.pallas_call(
        functools.partial(second_kernel, width=width),
        grid=(ranks,),
        out_shape=(
            jax.ShapeDtypeStruct((ranks, total_z, lanes), F32),
            jax.ShapeDtypeStruct((ranks, width, lanes), F32),
            jax.ShapeDtypeStruct((gram_rows, 128), F32),
        ),
        in_specs=[
            pl.BlockSpec((parts, groups, 1, cols_z, lanes), lambda i: (0, 0, i, 0, 0)),
            pl.BlockSpec((width, total_z), lambda i: (0, 0)),
        ],
        out_specs=(
            pl.BlockSpec((1, total_z, lanes), lambda i: (i, 0, 0)),
            pl.BlockSpec((1, width, lanes), lambda i: (i, 0, 0)),
            pl.BlockSpec((gram_rows, 128), lambda i: (0, 0)),
        ),
        scratch_shapes=[pltpu.VMEM((width, -(-width // 128) * 128), F32)],
        compiler_params=pltpu.CompilerParams(vmem_limit_bytes=VMEM_LIMIT),
        name="second_stage",
    )(recv, test_t)


def middle_kernel(gram_ref, second_ref, core_ref, q_ref, sums_ref, inv_ref, wide_ref, *, width):
    tiles = [
        [gram_ref[8 * t : 8 * t + 8, :], gram_ref[width + 8 * t : width + 8 * t + 8, :]]
        for t in range(width // 8)
    ]
    put_inverse(tiles, width, inv_ref)
    inv = inv_ref[:, :width]
    total_z = core_ref.shape[1]
    gram = None
    last = None
    for r in range(second_ref.shape[0]):
        q = mm(inv, second_ref[r])
        q_ref[r] = q
        g = mm_nt(q, q)
        h = mm_nt(q, core_ref[r])
        gram = g if gram is None else gram + g
        last = h if last is None else last + h
    wide_ref[:, total_z:] = jnp.zeros((width, wide_ref.shape[1] - total_z), F32)
    wide_ref[:, :total_z] = last
    wide_ref[:, total_z : total_z + width] = gram
    lanes = wide_ref.shape[1] // 128
    for t in range(width // 8):
        for l in range(lanes):
            sums_ref[t * lanes + l] = wide_ref[8 * t : 8 * t + 8, 128 * l : 128 * l + 128]
    for n in range(width // 8 * lanes, sums_ref.shape[0]):
        sums_ref[n] = jnp.zeros((8, 128), F32)


def middle_stage(gram, second, core, devices):
    import functools

    ranks, width, lanes = second.shape
    total_z = core.shape[1]
    wide = total_z + -(-width // 128) * 128
    count = width // 8 * (wide // 128)
    count = -(-count // devices) * devices
    vmem = pl.BlockSpec(memory_space=pltpu.VMEM)
    return pl.pallas_call(
        functools.partial(middle_kernel, width=width),
        out_shape=(
            jax.ShapeDtypeStruct((ranks, width, lanes), F32),
            jax.ShapeDtypeStruct((count, 8, 128), F32),
        ),
        in_specs=[vmem, vmem, vmem],
        out_specs=(vmem, vmem),
        scratch_shapes=[
            pltpu.VMEM((width, -(-width // 128) * 128), F32),
            pltpu.VMEM((width, wide), F32),
        ],
        compiler_params=pltpu.CompilerParams(vmem_limit_bytes=VMEM_LIMIT),
        name="middle_stage",
    )(gram, second, core)


def last_kernel(sums_ref, q_ref, basis_ref, last_ref, inv_ref, wide_ref, *, width, lanes, scales):
    first = last_ref.shape[1] // 128
    tiles = [
        [sums_ref[t * lanes + first + l] for l in range(lanes - first)] for t in range(width // 8)
    ]
    put_inverse(tiles, width, inv_ref)
    inv = inv_ref[:, :width]
    for t in range(width // 8):
        for l in range(first):
            wide_ref[8 * t : 8 * t + 8, 128 * l : 128 * l + 128] = sums_ref[t * lanes + l]
    last_ref[...] = scales[1] * mm(inv, wide_ref[...])
    for r in range(q_ref.shape[0]):
        basis = scales[0] * mm(inv, q_ref[r])
        basis = basis.T
        for m in range(basis_ref.shape[0]):
            rows = basis_ref.shape[2]
            basis_ref[m, r] = basis[m * rows : (m + 1) * rows, :]


def last_stage(sums, q, total_z, members, scales):
    import functools

    ranks, width, span = q.shape
    lanes = (total_z + -(-width // 128) * 128) // 128
    vmem = pl.BlockSpec(memory_space=pltpu.VMEM)
    return pl.pallas_call(
        functools.partial(last_kernel, width=width, lanes=lanes, scales=scales),
        out_shape=(
            jax.ShapeDtypeStruct((members, ranks, span // members, width), F32),
            jax.ShapeDtypeStruct((width, total_z), F32),
        ),
        in_specs=[vmem, vmem],
        out_specs=(vmem, vmem),
        scratch_shapes=[
            pltpu.VMEM((width, -(-width // 128) * 128), F32),
            pltpu.VMEM((width, total_z), F32),
        ],
        compiler_params=pltpu.CompilerParams(vmem_limit_bytes=VMEM_LIMIT),
        name="last_stage",
    )(sums, q)


def swap(pieces, axes, groups=None):
    return lax.all_to_all(pieces, axes, 0, 0, axis_index_groups=groups, tiled=True)


def share(piece, axes, count):
    return swap(jnp.broadcast_to(piece[None], (count,) + piece.shape), axes)


def shards(tensor, factor_y, factor_z, test_matrix):
    rows_x, cols_z, cols_y = tensor.shape
    rank = factor_y.shape[1]
    width = test_matrix.shape[1]
    n_sx = lax.axis_size("sx")
    n_ly = lax.axis_size("ly")
    both = ("sx", "ly")
    devices = n_sx * n_ly
    total_x = rows_x * n_sx
    total_z = cols_z * n_ly
    partial_value = jnp.dot(tensor.reshape(rows_x * cols_z, cols_y), factor_y, precision=HI)
    partial_value = partial_value.reshape(rows_x, cols_z, rank)
    local_sketch = jnp.sum(partial_value * factor_z[None], axis=1)
    mine = jnp.sum(swap(local_sketch.reshape(n_ly, rows_x // n_ly, rank), "ly"), axis=0)
    sketch = share(mine, both, devices).reshape(total_x, rank)
    index = lax.axis_index("sx").astype(jnp.int32).reshape(1)
    qt, basis_t = first_basis(sketch, index, rows_x, math.sqrt(total_x))

    blocks = cols_y // 128
    members = n_ly // blocks
    ranks = rank // (n_sx * members)
    partial_core = product(qt, tensor, n_sx)
    recv = swap(partial_core.reshape(devices, ranks, cols_z, 128), both)
    recv = recv.reshape(n_sx, n_ly, ranks, cols_z, 128)
    core, second, gram = second_stage(recv, test_matrix.T, devices)
    gram = jnp.sum(swap(gram.reshape(devices, 4, 128), both), axis=0)
    gram = share(gram, both, devices).reshape(devices * 4, 128)
    q_one, sums = middle_stage(gram, second, core, devices)
    per = sums.shape[0] // devices
    sums = jnp.sum(swap(sums.reshape(devices, per, 8, 128), both), axis=0)
    sums = share(sums, both, devices).reshape(devices * per, 8, 128)
    scales = (math.sqrt(rank * cols_y), math.sqrt(width / (total_x * cols_y)))
    basis, last_core = last_stage(sums, q_one, total_z, members, scales)
    groups = [[b * members + m for m in range(members)] for b in range(blocks)]
    basis = swap(basis, "ly", groups)
    basis_second = basis.reshape(members * ranks, 128 // members, width)
    return (basis_t.T, basis_second, last_core)


def solution(mesh):
    return jax.shard_map(
        shards,
        mesh=mesh,
        in_specs=(P("sx", "ly", None), P(), P("ly", None), P()),
        out_specs=(P("sx", None), P("sx", "ly", None), P()),
        check_vma=False,
    )
```

```python
import functools
import math

import jax
import jax.numpy as jnp
from jax import lax
from jax.experimental import pallas as pl
from jax.experimental.pallas import tpu as pltpu
from jax.sharding import PartitionSpec as P

HI = lax.Precision.HIGHEST
F32 = jnp.float32
VMEM_LIMIT = 56 * 1024 * 1024
UNROLL = 4


GROUP = 5


def tiles_of(ref, size, row0=0):
    lanes = -(-size // 128)
    return [
        [ref[row0 + 8 * t : row0 + 8 * t + 8, 128 * l : 128 * l + 128] for l in range(lanes)]
        for t in range(size // 8)
    ]


def spread(row, tile):
    return jnp.broadcast_to(tile[row : row + 1, :], (8, 128))


def put_inverse(tiles, size, out_ref, group=GROUP):
    count = size // 8
    lanes = -(-size // 128)
    lane = lax.broadcasted_iota(jnp.int32, (8, 128), 1)
    sub = lax.broadcasted_iota(jnp.int32, (8, 128), 0)
    work = [list(r) for r in tiles]
    for g in range(0, count, group):
        end = min(g + group, count)
        done = []
        for p in range(g, end):
            l0, c0 = divmod(8 * p, 128)
            span = range(p, end)
            cols = {t: [jnp.broadcast_to(work[t][l0][:, c0 + i : c0 + i + 1], (8, 128)) for i in range(8)] for t in span}
            block = list(cols[p])
            unit = [jnp.where(sub == c, 1.0, 0.0) for c in range(8)]
            diag = None
            for i in range(8):
                diag = block[i] if i == 0 else jnp.where(sub == i, block[i], diag)
                if i == 7:
                    break
                factor = block[i] * spread(i, 1.0 / block[i])
                factor = jnp.where(sub > i, factor, 0.0)
                for m in range(i + 1, 8):
                    block[m] = block[m] - factor * spread(i, block[m])
                for c in range(i + 1):
                    unit[c] = unit[c] - factor * spread(i, unit[c])
            root = lax.rsqrt(diag)
            root = root * (1.5 - 0.5 * diag * root * root)
            inv = [u * root for u in unit]
            src = list(work[p])
            inside = (lane >= c0) & (lane < c0 + 8)
            src[l0] = jnp.where(inside, jnp.where(lane - c0 == sub, 1.0, 0.0), src[l0])
            rows = []
            for l in range(lanes):
                terms = [inv[i] * spread(i, src[l]) for i in range(8)]
                rows.append(((terms[0] + terms[1]) + (terms[2] + terms[3])) + ((terms[4] + terms[5]) + (terms[6] + terms[7])))
            for l in range(lanes):
                pos = lane + 128 * l
                out_ref[8 * p : 8 * p + 8, 128 * l : 128 * l + 128] = jnp.where(pos <= sub + 8 * p, rows[l], 0.0)
            done.append(rows)
            for t in range(p + 1, end):
                factors = []
                for m in range(8):
                    terms = [cols[t][i] * spread(m, inv[i]) for i in range(m + 1)]
                    while len(terms) > 1:
                        terms = [a + b for a, b in zip(terms[::2], terms[1::2])] + ([terms[-1]] if len(terms) % 2 else [])
                    factors.append(terms[0])
                for l in range(lanes):
                    old = work[t][l]
                    if l == l0:
                        old = jnp.where(inside, 0.0, old)
                    terms = [factors[m] * spread(m, rows[l]) for m in range(8)]
                    work[t][l] = old - (((terms[0] + terms[1]) + (terms[2] + terms[3])) + ((terms[4] + terms[5]) + (terms[6] + terms[7])))
        if end < count:
            left = jnp.concatenate([jnp.concatenate(r, axis=1) for r in done], axis=0)
            pos = lax.broadcasted_iota(jnp.int32, left.shape, 1)
            own = lax.broadcasted_iota(jnp.int32, left.shape, 0) + 8 * g
            right = jnp.where((pos > own) & (pos < 8 * end), 0.0, left)
            outer = lax.dot_general(left, right, (((0,), (0,)), ((), ())), precision=HI, preferred_element_type=F32)
            for t in range(end, count):
                for l in range(lanes):
                    pos = lane + 128 * l
                    old = work[t][l]
                    if 128 * l < 8 * end and 128 * l + 128 > 8 * g:
                        old = jnp.where((pos >= 8 * g) & (pos < 8 * end), 0.0, old)
                    work[t][l] = old - outer[8 * t : 8 * t + 8, 128 * l : 128 * l + 128]


def split(value):
    high = value.astype(jnp.bfloat16)
    rest = value - high.astype(F32)
    middle = rest.astype(jnp.bfloat16)
    low = (rest - middle.astype(F32)).astype(jnp.bfloat16)
    return high, middle, low


def dot_bf16(a, b):
    return lax.dot_general(a, b, (((1,), (0,)), ((), ())), preferred_element_type=F32)


def dot_six(a, b, transposed=False):
    rows = a.shape[0]
    dims = (((1,), (1 if transposed else 0,)), ((), ()))
    left = jnp.concatenate(split(a), axis=0)
    high, middle, low = split(b)

    def dot(x, y):
        return lax.dot_general(x, y, dims, preferred_element_type=F32)

    first = dot(left, high)
    second = dot(left[: 2 * rows], middle)
    third = dot(left[:rows], low)
    return first[:rows] + (
        (first[rows : 2 * rows] + second[:rows]) + (first[2 * rows :] + (second[rows:] + third))
    )


def first_kernel(index_ref, sketch_ref, q_ref, basis_ref, gram_ref, inv_ref, wide_ref, *, rank, scale):
    rows_x = q_ref.shape[1]
    total = wide_ref.shape[1]
    halves = rows_x // 128
    for n in range(total // 128):
        block, half = divmod(n, halves)
        rows = pl.ds(block * rank * halves + half, rank, stride=halves)
        wide_ref[:, 128 * n : 128 * n + 128] = sketch_ref[rows, :]
    gram_ref[...] = jnp.zeros_like(gram_ref)
    sketch = wide_ref[...]
    gram_ref[:, :rank] = dot_six(sketch, sketch, True)
    put_inverse(tiles_of(gram_ref, rank), rank, inv_ref)
    qt = dot_six(inv_ref[:, :rank], sketch)
    wide_ref[...] = qt
    gram_ref[:, :rank] = dot_six(qt, qt, True)
    put_inverse(tiles_of(gram_ref, rank), rank, inv_ref)
    at = pl.multiple_of(index_ref[0] * rows_x, 128)
    mine = dot_six(inv_ref[:, :rank], wide_ref[:, pl.ds(at, rows_x)])
    q_ref[...] = mine
    basis_ref[...] = scale * mine


def first_basis(sketch, index, rank, rows_x, scale):
    total = sketch.shape[0] * 128 // rank
    wide = -(-rank // 128) * 128
    shape = jax.ShapeDtypeStruct((rank, rows_x), F32)
    vmem = pl.BlockSpec(memory_space=pltpu.VMEM)
    return pl.pallas_call(
        functools.partial(first_kernel, rank=rank, scale=scale),
        out_shape=(shape, shape),
        in_specs=[pl.BlockSpec(memory_space=pltpu.SMEM), vmem],
        out_specs=(vmem, vmem),
        scratch_shapes=[
            pltpu.VMEM((rank, wide), F32),
            pltpu.VMEM((rank, wide), F32),
            pltpu.VMEM((rank, total), F32),
        ],
        compiler_params=pltpu.CompilerParams(vmem_limit_bytes=VMEM_LIMIT),
        name="first_basis",
    )(index, sketch)


def sketch_kernel(*refs):
    slab_refs, (fy_ref, fz_ref, out_ref, left_ref, sum_ref) = refs[:-5], refs[-5:]
    step = pl.program_id(0)
    rows_x, span, lanes = slab_refs[0].shape
    rank = fy_ref.shape[0]
    flat = [ref.reshape(rows_x * span, lanes) for ref in slab_refs]

    @pl.when(step == 0)
    def _():
        for n, piece in enumerate(split(fy_ref[...])):
            left_ref[n * rank : (n + 1) * rank, :] = piece

    def dot(x, y):
        dims = (((1,), (1,)), ((), ()))
        return lax.dot_general(x, y, dims, preferred_element_type=F32)

    total = None
    for i in range(span):
        rows = pl.ds(i, rows_x, stride=span)
        high, middle, low = split(jnp.concatenate([ref[rows, :] for ref in flat], axis=1))
        first = dot(left_ref[...], high)
        second = dot(left_ref[: 2 * rank, :], middle)
        third = dot(left_ref[:rank, :], low)
        part = first[:rank] + (
            (first[rank : 2 * rank] + second[:rank]) + (first[2 * rank :] + (second[rank:] + third))
        )
        part = part * fz_ref[0, :, i : i + 1]
        total = part if total is None else total + part

    @pl.when(step == 0)
    def _():
        sum_ref[...] = total

    @pl.when(step > 0)
    def _():
        sum_ref[...] = sum_ref[...] + total

    @pl.when(step == pl.num_programs(0) - 1)
    def _():
        halves = rows_x // 128
        for n in range(halves):
            out_ref[pl.ds(n, rank, stride=halves), :] = sum_ref[:, 128 * n : 128 * n + 128]


def local_sketch(tensor, fy_t, factor_z):
    rows_x, cols_z, cols_y = tensor.shape
    rank = fy_t.shape[0]
    steps = cols_z // 8
    blocks = cols_y // 128
    fz = factor_z.reshape(steps, 8, rank).transpose(0, 2, 1)
    return pl.pallas_call(
        sketch_kernel,
        grid=(steps,),
        out_shape=jax.ShapeDtypeStruct((rank * rows_x // 128, 128), F32),
        in_specs=[
            *(
                pl.BlockSpec((rows_x, 8, 128), functools.partial(lambda l, i: (0, i, l), l))
                for l in range(blocks)
            ),
            pl.BlockSpec((rank, cols_y), lambda i: (0, 0)),
            pl.BlockSpec((1, rank, 8), lambda i: (i, 0, 0)),
        ],
        out_specs=pl.BlockSpec((rank * rows_x // 128, 128), lambda i: (0, 0)),
        scratch_shapes=[
            pltpu.VMEM((3 * rank, cols_y), jnp.bfloat16),
            pltpu.VMEM((rank, rows_x), F32),
        ],
        compiler_params=pltpu.CompilerParams(vmem_limit_bytes=VMEM_LIMIT),
        name="local_sketch",
    )(*[tensor] * blocks, fy_t, fz)


def product_kernel(qt_ref, slab_ref, out_ref, left_ref, *, cols_z, rows_x, parts, rank_part):
    rank = parts * rank_part

    @pl.when(pl.program_id(0) == 0)
    def _():
        for n, piece in enumerate(split(qt_ref[...])):
            left_ref[n * rank : (n + 1) * rank, :] = piece

    def body(step, carry):
        z = step * 2
        left = slab_ref[pl.ds(z, rows_x, stride=cols_z), :]
        right = slab_ref[pl.ds(z + 1, rows_x, stride=cols_z), :]
        high, middle, low = split(jnp.concatenate([left, right], axis=1))
        first = dot_bf16(left_ref[...], high)
        second = dot_bf16(left_ref[: 2 * rank, :], middle)
        third = dot_bf16(left_ref[:rank, :], low)
        both = first[:rank] + (
            (first[rank : 2 * rank] + second[:rank]) + (first[2 * rank :] + (second[rank:] + third))
        )
        for s in range(parts):
            piece = both[s * rank_part : (s + 1) * rank_part]
            out_ref[s, 0, pl.ds(z, rank_part, stride=cols_z), :] = piece[:, :128]
            out_ref[s, 0, pl.ds(z + 1, rank_part, stride=cols_z), :] = piece[:, 128:]
        return carry

    lax.fori_loop(0, cols_z // 2, body, 0, unroll=UNROLL)


def product(qt, tensor, parts):
    rows_x, cols_z, cols_y = tensor.shape
    rank = qt.shape[0]
    blocks = cols_y // 128
    rank_part = rank // parts
    flat = tensor.reshape(rows_x * cols_z, cols_y)
    return pl.pallas_call(
        functools.partial(
            product_kernel, cols_z=cols_z, rows_x=rows_x, parts=parts, rank_part=rank_part
        ),
        grid=(blocks,),
        out_shape=jax.ShapeDtypeStruct((parts, blocks, rank_part * cols_z, 128), F32),
        in_specs=[
            pl.BlockSpec((rank, rows_x), lambda i: (0, 0)),
            pl.BlockSpec((rows_x * cols_z, 128), lambda i: (0, i)),
        ],
        out_specs=pl.BlockSpec((parts, 1, rank_part * cols_z, 128), lambda i: (0, i, 0, 0)),
        scratch_shapes=[pltpu.VMEM((3 * rank, rows_x), jnp.bfloat16)],
        compiler_params=pltpu.CompilerParams(vmem_limit_bytes=VMEM_LIMIT),
        name="product",
    )(qt, flat)


def second_kernel(recv_ref, test_ref, core_ref, second_ref, gram_out_ref, gram_ref, *, width):
    step = pl.program_id(0)
    core = recv_ref[0, :, 0] + recv_ref[1, :, 0]
    core = core + (recv_ref[2, :, 0] + recv_ref[3, :, 0])
    core = core.reshape(core_ref.shape)
    core_ref[...] = core
    sec = dot_six(test_ref[...], core)
    second_ref[...] = sec
    part = dot_six(sec, sec, True)

    @pl.when(step == 0)
    def _():
        gram_ref[:, :width] = part

    @pl.when(step > 0)
    def _():
        gram_ref[:, :width] = gram_ref[:, :width] + part

    @pl.when(step == pl.num_programs(0) - 1)
    def _():
        gram_out_ref[...] = jnp.zeros_like(gram_out_ref)
        gram_out_ref[:width, :] = gram_ref[:, :128]
        gram_out_ref[width : 2 * width, : width - 128] = gram_ref[:, 128:width]


def second_stage(recv, test_t, devices):
    parts, groups, ranks, cols_z, lanes = recv.shape
    width, total_z = test_t.shape
    gram_rows = 4 * devices
    return pl.pallas_call(
        functools.partial(second_kernel, width=width),
        grid=(ranks,),
        out_shape=(
            jax.ShapeDtypeStruct((total_z, ranks * lanes), F32),
            jax.ShapeDtypeStruct((width, ranks * lanes), F32),
            jax.ShapeDtypeStruct((gram_rows, 128), F32),
        ),
        in_specs=[
            pl.BlockSpec((parts, groups, 1, cols_z, lanes), lambda i: (0, 0, i, 0, 0)),
            pl.BlockSpec((width, total_z), lambda i: (0, 0)),
        ],
        out_specs=(
            pl.BlockSpec((total_z, lanes), lambda i: (0, i)),
            pl.BlockSpec((width, lanes), lambda i: (0, i)),
            pl.BlockSpec((gram_rows, 128), lambda i: (0, 0)),
        ),
        scratch_shapes=[pltpu.VMEM((width, -(-width // 128) * 128), F32)],
        compiler_params=pltpu.CompilerParams(vmem_limit_bytes=VMEM_LIMIT),
        name="second_stage",
    )(recv, test_t)


def middle_kernel(gram_ref, second_ref, core_ref, q_ref, sums_ref, inv_ref, wide_ref, *, width):
    tiles = [
        [gram_ref[8 * t : 8 * t + 8, :], gram_ref[width + 8 * t : width + 8 * t + 8, :]]
        for t in range(width // 8)
    ]
    put_inverse(tiles, width, inv_ref)
    total_z = core_ref.shape[0]
    q = dot_six(inv_ref[:, :width], second_ref[...])
    members, ranks, rows, _ = q_ref.shape
    for r in range(ranks):
        turned = q[:, r * members * rows : (r + 1) * members * rows].T
        for m in range(members):
            q_ref[m, r] = turned[m * rows : (m + 1) * rows, :]
    wide_ref[:, total_z:] = jnp.zeros((width, wide_ref.shape[1] - total_z), F32)
    wide_ref[:, :total_z] = dot_six(q, core_ref[...], True)
    wide_ref[:, total_z : total_z + width] = dot_six(q, q, True)
    lanes = wide_ref.shape[1] // 128
    for t in range(width // 8):
        for l in range(lanes):
            sums_ref[t * lanes + l] = wide_ref[8 * t : 8 * t + 8, 128 * l : 128 * l + 128]
    for n in range(width // 8 * lanes, sums_ref.shape[0]):
        sums_ref[n] = jnp.zeros((8, 128), F32)


def middle_stage(gram, second, core, devices, ranks, members):
    width, pairs = second.shape
    total_z = core.shape[0]
    wide = total_z + -(-width // 128) * 128
    count = width // 8 * (wide // 128)
    count = -(-count // devices) * devices
    vmem = pl.BlockSpec(memory_space=pltpu.VMEM)
    return pl.pallas_call(
        functools.partial(middle_kernel, width=width),
        out_shape=(
            jax.ShapeDtypeStruct((members, ranks, pairs // ranks // members, width), F32),
            jax.ShapeDtypeStruct((count, 8, 128), F32),
        ),
        in_specs=[vmem, vmem, vmem],
        out_specs=(vmem, vmem),
        scratch_shapes=[
            pltpu.VMEM((width, -(-width // 128) * 128), F32),
            pltpu.VMEM((width, wide), F32),
        ],
        compiler_params=pltpu.CompilerParams(vmem_limit_bytes=VMEM_LIMIT),
        name="middle_stage",
    )(gram, second, core)


def last_kernel(sums_ref, last_ref, inv_ref, wide_ref, *, width, lanes, scale):
    first = last_ref.shape[1] // 128
    tiles = [
        [sums_ref[t * lanes + first + l] for l in range(lanes - first)] for t in range(width // 8)
    ]
    put_inverse(tiles, width, inv_ref)
    for t in range(width // 8):
        for l in range(first):
            wide_ref[8 * t : 8 * t + 8, 128 * l : 128 * l + 128] = sums_ref[t * lanes + l]
    last_ref[...] = scale * dot_six(inv_ref[:, :width], wide_ref[...])


def last_stage(sums, total_z, width, scale):
    wide = -(-width // 128) * 128
    vmem = pl.BlockSpec(memory_space=pltpu.VMEM)
    return pl.pallas_call(
        functools.partial(last_kernel, width=width, lanes=(total_z + wide) // 128, scale=scale),
        out_shape=(
            jax.ShapeDtypeStruct((width, total_z), F32),
            jax.ShapeDtypeStruct((width, wide), F32),
        ),
        in_specs=[vmem],
        out_specs=(vmem, vmem),
        scratch_shapes=[pltpu.VMEM((width, total_z), F32)],
        compiler_params=pltpu.CompilerParams(vmem_limit_bytes=VMEM_LIMIT),
        name="last_stage",
    )(sums)


def basis_kernel(q_ref, inv_ref, basis_ref, *, scale):
    basis_ref[...] = scale * dot_six(q_ref[...], inv_ref[:, : q_ref.shape[1]], True)


def basis_stage(q, inverse, scale):
    vmem = pl.BlockSpec(memory_space=pltpu.VMEM)
    return pl.pallas_call(
        functools.partial(basis_kernel, scale=scale),
        out_shape=jax.ShapeDtypeStruct(q.shape, F32),
        in_specs=[vmem, vmem],
        out_specs=vmem,
        compiler_params=pltpu.CompilerParams(vmem_limit_bytes=VMEM_LIMIT),
        name="basis_stage",
    )(q, inverse)


def swap(pieces, axes, groups=None):
    return lax.all_to_all(pieces, axes, 0, 0, axis_index_groups=groups, tiled=True)


def share(piece, axes, count):
    return swap(jnp.broadcast_to(piece[None], (count,) + piece.shape), axes)


def shards(tensor, factor_y, factor_z, test_matrix):
    rows_x, cols_z, cols_y = tensor.shape
    rank = factor_y.shape[1]
    width = test_matrix.shape[1]
    n_sx = lax.axis_size("sx")
    n_ly = lax.axis_size("ly")
    both = ("sx", "ly")
    devices = n_sx * n_ly
    total_x = rows_x * n_sx
    total_z = cols_z * n_ly
    halves = rows_x // 128
    local = local_sketch(tensor, factor_y.T, factor_z)
    local = swap(local.reshape(rank, halves, 128), "ly")
    mine = jnp.sum(local.reshape(n_ly, rank // n_ly, halves, 128), axis=0)
    sketch = share(mine, both, devices).reshape(n_sx * rank * halves, 128)
    index = lax.axis_index("sx").astype(jnp.int32).reshape(1)
    qt, basis_t = first_basis(sketch, index, rank, rows_x, math.sqrt(total_x))

    blocks = cols_y // 128
    members = n_ly // blocks
    ranks = rank // (n_sx * members)
    partial_core = product(qt, tensor, n_sx)
    recv = swap(partial_core.reshape(devices, ranks, cols_z, 128), both)
    recv = recv.reshape(n_sx, n_ly, ranks, cols_z, 128)
    core, second, gram = second_stage(recv, test_matrix.T, devices)
    gram = jnp.sum(swap(gram.reshape(devices, 4, 128), both), axis=0)
    gram = share(gram, both, devices).reshape(devices * 4, 128)
    q_one, sums = middle_stage(gram, second, core, devices, ranks, members)
    groups = [[b * members + m for m in range(members)] for b in range(blocks)]
    q_mine = swap(q_one, "ly", groups)
    q_mine = q_mine.reshape(rank // n_sx * (128 // members), width)
    per = sums.shape[0] // devices
    sums = swap(sums.reshape(devices, per, 8, 128), both)
    sums = jnp.sum(sums, axis=0)
    sums = share(sums, both, devices)
    sums = sums.reshape(devices * per, 8, 128)
    core_scale = math.sqrt(width / (total_x * cols_y))
    last_core, inverse = last_stage(sums, total_z, width, core_scale)
    basis = basis_stage(q_mine, inverse, math.sqrt(rank * cols_y))
    basis_second = basis.reshape(rank // n_sx, 128 // members, width)
    return (basis_t.T, basis_second, last_core)


def solution(mesh):
    return jax.shard_map(
        shards,
        mesh=mesh,
        in_specs=(P("sx", "ly", None), P(), P("ly", None), P()),
        out_specs=(P("sx", None), P("sx", "ly", None), P()),
        check_vma=False,
    )
```

```python
import functools
import math

import jax
import jax.numpy as jnp
from jax import lax
from jax.experimental import pallas as pl
from jax.experimental.pallas import tpu as pltpu
from jax.sharding import PartitionSpec as P

HI = lax.Precision.HIGHEST
F32 = jnp.float32
VMEM_LIMIT = 56 * 1024 * 1024
UNROLL = 10


GROUP = 10


def tiles_of(ref, size, row0=0):
    lanes = -(-size // 128)
    return [
        [ref[row0 + 8 * t : row0 + 8 * t + 8, 128 * l : 128 * l + 128] for l in range(lanes)]
        for t in range(size // 8)
    ]


def spread(row, tile):
    return jnp.broadcast_to(tile[row : row + 1, :], (8, 128))


def put_inverse(tiles, size, out_ref, group=GROUP):
    count = size // 8
    lanes = -(-size // 128)
    lane = lax.broadcasted_iota(jnp.int32, (8, 128), 1)
    sub = lax.broadcasted_iota(jnp.int32, (8, 128), 0)
    work = [list(r) for r in tiles]
    for g in range(0, count, group):
        end = min(g + group, count)
        done = []
        for p in range(g, end):
            l0, c0 = divmod(8 * p, 128)
            span = range(p, end)
            cols = {t: [jnp.broadcast_to(work[t][l0][:, c0 + i : c0 + i + 1], (8, 128)) for i in range(8)] for t in span}
            block = list(cols[p])
            unit = [jnp.where(sub == c, 1.0, 0.0) for c in range(8)]
            diag = None
            for i in range(8):
                diag = block[i] if i == 0 else jnp.where(sub == i, block[i], diag)
                if i == 7:
                    break
                factor = block[i] * spread(i, 1.0 / block[i])
                for m in range(i + 1, 8):
                    block[m] = block[m] - factor * spread(i, block[m])
                factor = jnp.where(sub > i, factor, 0.0)
                for c in range(i + 1):
                    unit[c] = unit[c] - factor * spread(i, unit[c])
            root = lax.rsqrt(diag)
            root = root * (1.5 - 0.5 * diag * root * root)
            inv = [u * root for u in unit]
            src = list(work[p])
            inside = (lane >= c0) & (lane < c0 + 8)
            src[l0] = jnp.where(inside, jnp.where(lane - c0 == sub, 1.0, 0.0), src[l0])
            rows = []
            for l in range(lanes):
                terms = [inv[i] * spread(i, src[l]) for i in range(8)]
                rows.append(((terms[0] + terms[1]) + (terms[2] + terms[3])) + ((terms[4] + terms[5]) + (terms[6] + terms[7])))
            for l in range(lanes):
                pos = lane + 128 * l
                out_ref[8 * p : 8 * p + 8, 128 * l : 128 * l + 128] = jnp.where(pos <= sub + 8 * p, rows[l], 0.0)
            done.append(rows)
            for t in range(p + 1, end):
                factors = []
                for m in range(8):
                    terms = [cols[t][i] * spread(m, inv[i]) for i in range(m + 1)]
                    while len(terms) > 1:
                        terms = [a + b for a, b in zip(terms[::2], terms[1::2])] + ([terms[-1]] if len(terms) % 2 else [])
                    factors.append(terms[0])
                for l in range(lanes):
                    old = work[t][l]
                    if l == l0:
                        old = jnp.where(inside, 0.0, old)
                    terms = [factors[m] * spread(m, rows[l]) for m in range(8)]
                    work[t][l] = old - (((terms[0] + terms[1]) + (terms[2] + terms[3])) + ((terms[4] + terms[5]) + (terms[6] + terms[7])))
        if end < count:
            left = jnp.concatenate([jnp.concatenate(r, axis=1) for r in done], axis=0)
            pos = lax.broadcasted_iota(jnp.int32, left.shape, 1)
            own = lax.broadcasted_iota(jnp.int32, left.shape, 0) + 8 * g
            right = jnp.where((pos > own) & (pos < 8 * end), 0.0, left)
            outer = lax.dot_general(left, right, (((0,), (0,)), ((), ())), precision=HI, preferred_element_type=F32)
            for t in range(end, count):
                for l in range(lanes):
                    pos = lane + 128 * l
                    old = work[t][l]
                    if 128 * l < 8 * end and 128 * l + 128 > 8 * g:
                        old = jnp.where((pos >= 8 * g) & (pos < 8 * end), 0.0, old)
                    work[t][l] = old - outer[8 * t : 8 * t + 8, 128 * l : 128 * l + 128]


def split(value):
    high = value.astype(jnp.bfloat16)
    rest = value - high.astype(F32)
    middle = rest.astype(jnp.bfloat16)
    low = (rest - middle.astype(F32)).astype(jnp.bfloat16)
    return high, middle, low


def dot_bf16(a, b):
    return lax.dot_general(a, b, (((1,), (0,)), ((), ())), preferred_element_type=F32)


def dot_six(a, b, transposed=False):
    rows = a.shape[0]
    dims = (((1,), (1 if transposed else 0,)), ((), ()))
    left = jnp.concatenate(split(a), axis=0)
    high, middle, low = split(b)

    def dot(x, y):
        return lax.dot_general(x, y, dims, preferred_element_type=F32)

    first = dot(left, high)
    second = dot(left[: 2 * rows], middle)
    third = dot(left[:rows], low)
    return first[:rows] + (
        (first[rows : 2 * rows] + second[:rows]) + (first[2 * rows :] + (second[rows:] + third))
    )


def first_kernel(index_ref, sketch_ref, q_ref, basis_ref, gram_ref, inv_ref, wide_ref, *, rank, scale):
    rows_x = q_ref.shape[1]
    total = wide_ref.shape[1]
    halves = rows_x // 128
    for n in range(total // 128):
        block, half = divmod(n, halves)
        rows = pl.ds(block * rank * halves + half, rank, stride=halves)
        wide_ref[:, 128 * n : 128 * n + 128] = sketch_ref[rows, :]
    gram_ref[...] = jnp.zeros_like(gram_ref)
    sketch = wide_ref[...]
    gram_ref[:, :rank] = dot_six(sketch, sketch, True)
    put_inverse(tiles_of(gram_ref, rank), rank, inv_ref)
    qt = dot_six(inv_ref[:, :rank], sketch)
    wide_ref[...] = qt
    gram_ref[:, :rank] = dot_six(qt, qt, True)
    put_inverse(tiles_of(gram_ref, rank), rank, inv_ref)
    at = pl.multiple_of(index_ref[0] * rows_x, 128)
    mine = dot_six(inv_ref[:, :rank], wide_ref[:, pl.ds(at, rows_x)])
    q_ref[...] = mine
    basis_ref[...] = scale * mine


def first_basis(sketch, index, rank, rows_x, scale):
    total = sketch.shape[0] * 128 // rank
    wide = -(-rank // 128) * 128
    shape = jax.ShapeDtypeStruct((rank, rows_x), F32)
    vmem = pl.BlockSpec(memory_space=pltpu.VMEM)
    return pl.pallas_call(
        functools.partial(first_kernel, rank=rank, scale=scale),
        out_shape=(shape, shape),
        in_specs=[pl.BlockSpec(memory_space=pltpu.SMEM), vmem],
        out_specs=(vmem, vmem),
        scratch_shapes=[
            pltpu.VMEM((rank, wide), F32),
            pltpu.VMEM((rank, wide), F32),
            pltpu.VMEM((rank, total), F32),
        ],
        compiler_params=pltpu.CompilerParams(vmem_limit_bytes=VMEM_LIMIT),
        name="first_basis",
    )(index, sketch)


def sketch_kernel(*refs):
    slab_refs, (fy_ref, fz_ref, out_ref, left_ref, sum_ref) = refs[:-5], refs[-5:]
    step = pl.program_id(0)
    rows_x, span, lanes = slab_refs[0].shape
    rank = fy_ref.shape[0]
    flat = [ref.reshape(rows_x * span, lanes) for ref in slab_refs]

    @pl.when(step == 0)
    def _():
        for n, piece in enumerate(split(fy_ref[...])):
            left_ref[n * rank : (n + 1) * rank, :] = piece

    def dot(x, y):
        dims = (((1,), (1,)), ((), ()))
        return lax.dot_general(x, y, dims, preferred_element_type=F32)

    turned = fz_ref[...].T
    total = None
    for i in range(span):
        rows = pl.ds(i, rows_x, stride=span)
        high, middle, low = split(jnp.concatenate([ref[rows, :] for ref in flat], axis=1))
        first = dot(left_ref[...], high)
        second = dot(left_ref[: 2 * rank, :], middle)
        third = dot(left_ref[:rank, :], low)
        part = first[:rank] + (
            (first[rank : 2 * rank] + second[:rank]) + (first[2 * rank :] + (second[rank:] + third))
        )
        part = part * turned[:, i : i + 1]
        total = part if total is None else total + part

    @pl.when(step == 0)
    def _():
        sum_ref[...] = total

    @pl.when(step > 0)
    def _():
        sum_ref[...] = sum_ref[...] + total

    @pl.when(step == pl.num_programs(0) - 1)
    def _():
        halves = rows_x // 128
        for n in range(halves):
            out_ref[pl.ds(n, rank, stride=halves), :] = sum_ref[:, 128 * n : 128 * n + 128]


def local_sketch(tensor, fy_t, factor_z):
    rows_x, cols_z, cols_y = tensor.shape
    rank = fy_t.shape[0]
    steps = cols_z // 8
    blocks = cols_y // 128
    return pl.pallas_call(
        sketch_kernel,
        grid=(steps,),
        out_shape=jax.ShapeDtypeStruct((rank * rows_x // 128, 128), F32),
        in_specs=[
            *(
                pl.BlockSpec((rows_x, 8, 128), functools.partial(lambda l, i: (0, i, l), l))
                for l in range(blocks)
            ),
            pl.BlockSpec((rank, cols_y), lambda i: (0, 0)),
            pl.BlockSpec((8, rank), lambda i: (i, 0)),
        ],
        out_specs=pl.BlockSpec((rank * rows_x // 128, 128), lambda i: (0, 0)),
        scratch_shapes=[
            pltpu.VMEM((3 * rank, cols_y), jnp.bfloat16),
            pltpu.VMEM((rank, rows_x), F32),
        ],
        compiler_params=pltpu.CompilerParams(vmem_limit_bytes=VMEM_LIMIT),
        name="local_sketch",
    )(*[tensor] * blocks, fy_t, factor_z)


def product_kernel(qt_ref, slab_ref, out_ref, left_ref, *, cols_z, rows_x, parts, rank_part):
    rank = parts * rank_part

    @pl.when(pl.program_id(0) == 0)
    def _():
        for n, piece in enumerate(split(qt_ref[...])):
            left_ref[n * rank : (n + 1) * rank, :] = piece

    def body(step, carry):
        z = step * 2
        left = slab_ref[pl.ds(z, rows_x, stride=cols_z), :]
        right = slab_ref[pl.ds(z + 1, rows_x, stride=cols_z), :]
        high, middle, low = split(jnp.concatenate([left, right], axis=1))
        first = dot_bf16(left_ref[...], high)
        second = dot_bf16(left_ref[: 2 * rank, :], middle)
        third = dot_bf16(left_ref[:rank, :], low)
        both = first[:rank] + (
            (first[rank : 2 * rank] + second[:rank]) + (first[2 * rank :] + (second[rank:] + third))
        )
        for s in range(parts):
            piece = both[s * rank_part : (s + 1) * rank_part]
            out_ref[s, 0, pl.ds(z, rank_part, stride=cols_z), :] = piece[:, :128]
            out_ref[s, 0, pl.ds(z + 1, rank_part, stride=cols_z), :] = piece[:, 128:]
        return carry

    lax.fori_loop(0, cols_z // 2, body, 0, unroll=UNROLL)


def product(qt, tensor, parts):
    rows_x, cols_z, cols_y = tensor.shape
    rank = qt.shape[0]
    blocks = cols_y // 128
    rank_part = rank // parts
    flat = tensor.reshape(rows_x * cols_z, cols_y)
    return pl.pallas_call(
        functools.partial(
            product_kernel, cols_z=cols_z, rows_x=rows_x, parts=parts, rank_part=rank_part
        ),
        grid=(blocks,),
        out_shape=jax.ShapeDtypeStruct((parts, blocks, rank_part * cols_z, 128), F32),
        in_specs=[
            pl.BlockSpec((rank, rows_x), lambda i: (0, 0)),
            pl.BlockSpec((rows_x * cols_z, 128), lambda i: (0, i)),
        ],
        out_specs=pl.BlockSpec((parts, 1, rank_part * cols_z, 128), lambda i: (0, i, 0, 0)),
        scratch_shapes=[pltpu.VMEM((3 * rank, rows_x), jnp.bfloat16)],
        compiler_params=pltpu.CompilerParams(vmem_limit_bytes=VMEM_LIMIT),
        name="product",
    )(qt, flat)


def second_kernel(recv_ref, test_ref, core_ref, second_ref, gram_out_ref, gram_ref, *, width):
    step = pl.program_id(0)
    core = recv_ref[0, :, 0] + recv_ref[1, :, 0]
    core = core + (recv_ref[2, :, 0] + recv_ref[3, :, 0])
    core = core.reshape(core_ref.shape)
    core_ref[...] = core
    sec = dot_six(test_ref[...], core)
    second_ref[...] = sec
    part = dot_six(sec, sec, True)

    @pl.when(step == 0)
    def _():
        gram_ref[:, :width] = part

    @pl.when(step > 0)
    def _():
        gram_ref[:, :width] = gram_ref[:, :width] + part

    @pl.when(step == pl.num_programs(0) - 1)
    def _():
        gram_out_ref[...] = jnp.zeros_like(gram_out_ref)
        gram_out_ref[:width, :] = gram_ref[:, :128]
        gram_out_ref[width : 2 * width, : width - 128] = gram_ref[:, 128:width]


def second_stage(recv, test_t, devices):
    parts, groups, ranks, cols_z, lanes = recv.shape
    width, total_z = test_t.shape
    gram_rows = 4 * devices
    return pl.pallas_call(
        functools.partial(second_kernel, width=width),
        grid=(ranks,),
        out_shape=(
            jax.ShapeDtypeStruct((total_z, ranks * lanes), F32),
            jax.ShapeDtypeStruct((width, ranks * lanes), F32),
            jax.ShapeDtypeStruct((gram_rows, 128), F32),
        ),
        in_specs=[
            pl.BlockSpec((parts, groups, 1, cols_z, lanes), lambda i: (0, 0, i, 0, 0)),
            pl.BlockSpec((width, total_z), lambda i: (0, 0)),
        ],
        out_specs=(
            pl.BlockSpec((total_z, lanes), lambda i: (0, i)),
            pl.BlockSpec((width, lanes), lambda i: (0, i)),
            pl.BlockSpec((gram_rows, 128), lambda i: (0, 0)),
        ),
        scratch_shapes=[pltpu.VMEM((width, -(-width // 128) * 128), F32)],
        compiler_params=pltpu.CompilerParams(vmem_limit_bytes=VMEM_LIMIT),
        name="second_stage",
    )(recv, test_t)


def middle_kernel(gram_ref, second_ref, core_ref, q_ref, sums_ref, inv_ref, wide_ref, *, width):
    tiles = [
        [gram_ref[8 * t : 8 * t + 8, :], gram_ref[width + 8 * t : width + 8 * t + 8, :]]
        for t in range(width // 8)
    ]
    put_inverse(tiles, width, inv_ref)
    total_z = core_ref.shape[0]
    q = dot_six(inv_ref[:, :width], second_ref[...])
    members, ranks, rows, _ = q_ref.shape
    for r in range(ranks):
        turned = q[:, r * members * rows : (r + 1) * members * rows].T
        for m in range(members):
            q_ref[m, r] = turned[m * rows : (m + 1) * rows, :]
    wide_ref[:, total_z:] = jnp.zeros((width, wide_ref.shape[1] - total_z), F32)
    wide_ref[:, :total_z] = dot_six(q, core_ref[...], True)
    wide_ref[:, total_z : total_z + width] = dot_six(q, q, True)
    lanes = wide_ref.shape[1] // 128
    for t in range(width // 8):
        for l in range(lanes):
            sums_ref[t * lanes + l] = wide_ref[8 * t : 8 * t + 8, 128 * l : 128 * l + 128]
    for n in range(width // 8 * lanes, sums_ref.shape[0]):
        sums_ref[n] = jnp.zeros((8, 128), F32)


def middle_stage(gram, second, core, devices, ranks, members):
    width, pairs = second.shape
    total_z = core.shape[0]
    wide = total_z + -(-width // 128) * 128
    count = width // 8 * (wide // 128)
    count = -(-count // devices) * devices
    vmem = pl.BlockSpec(memory_space=pltpu.VMEM)
    return pl.pallas_call(
        functools.partial(middle_kernel, width=width),
        out_shape=(
            jax.ShapeDtypeStruct((members, ranks, pairs // ranks // members, width), F32),
            jax.ShapeDtypeStruct((count, 8, 128), F32),
        ),
        in_specs=[vmem, vmem, vmem],
        out_specs=(vmem, vmem),
        scratch_shapes=[
            pltpu.VMEM((width, -(-width // 128) * 128), F32),
            pltpu.VMEM((width, wide), F32),
        ],
        compiler_params=pltpu.CompilerParams(vmem_limit_bytes=VMEM_LIMIT),
        name="middle_stage",
    )(gram, second, core)


def last_kernel(sums_ref, last_ref, inv_ref, wide_ref, *, width, lanes, scale):
    first = last_ref.shape[1] // 128
    tiles = [
        [sums_ref[t * lanes + first + l] for l in range(lanes - first)] for t in range(width // 8)
    ]
    put_inverse(tiles, width, inv_ref)
    for t in range(width // 8):
        for l in range(first):
            wide_ref[8 * t : 8 * t + 8, 128 * l : 128 * l + 128] = sums_ref[t * lanes + l]
    last_ref[...] = scale * dot_six(inv_ref[:, :width], wide_ref[...])


def last_stage(sums, total_z, width, scale):
    wide = -(-width // 128) * 128
    vmem = pl.BlockSpec(memory_space=pltpu.VMEM)
    return pl.pallas_call(
        functools.partial(last_kernel, width=width, lanes=(total_z + wide) // 128, scale=scale),
        out_shape=(
            jax.ShapeDtypeStruct((width, total_z), F32),
            jax.ShapeDtypeStruct((width, wide), F32),
        ),
        in_specs=[vmem],
        out_specs=(vmem, vmem),
        scratch_shapes=[pltpu.VMEM((width, total_z), F32)],
        compiler_params=pltpu.CompilerParams(vmem_limit_bytes=VMEM_LIMIT),
        name="last_stage",
    )(sums)


def basis_kernel(q_ref, inv_ref, basis_ref, *, scale):
    basis_ref[...] = scale * dot_six(q_ref[...], inv_ref[:, : q_ref.shape[1]], True)


def basis_stage(q, inverse, scale):
    vmem = pl.BlockSpec(memory_space=pltpu.VMEM)
    return pl.pallas_call(
        functools.partial(basis_kernel, scale=scale),
        out_shape=jax.ShapeDtypeStruct(q.shape, F32),
        in_specs=[vmem, vmem],
        out_specs=vmem,
        compiler_params=pltpu.CompilerParams(vmem_limit_bytes=VMEM_LIMIT),
        name="basis_stage",
    )(q, inverse)


def swap(pieces, axes, groups=None):
    return lax.all_to_all(pieces, axes, 0, 0, axis_index_groups=groups, tiled=True)


def share(piece, axes, count):
    return swap(jnp.broadcast_to(piece[None], (count,) + piece.shape), axes)


def shards(tensor, factor_y, factor_z, test_matrix):
    rows_x, cols_z, cols_y = tensor.shape
    rank = factor_y.shape[1]
    width = test_matrix.shape[1]
    n_sx = lax.axis_size("sx")
    n_ly = lax.axis_size("ly")
    both = ("sx", "ly")
    devices = n_sx * n_ly
    total_x = rows_x * n_sx
    total_z = cols_z * n_ly
    halves = rows_x // 128
    local = local_sketch(tensor, factor_y.T, factor_z)
    local = swap(local.reshape(rank, halves, 128), "ly")
    mine = jnp.sum(local.reshape(n_ly, rank // n_ly, halves, 128), axis=0)
    sketch = share(mine, both, devices).reshape(n_sx * rank * halves, 128)
    index = lax.axis_index("sx").astype(jnp.int32).reshape(1)
    qt, basis_t = first_basis(sketch, index, rank, rows_x, math.sqrt(total_x))

    blocks = cols_y // 128
    members = n_ly // blocks
    ranks = rank // (n_sx * members)
    partial_core = product(qt, tensor, n_sx)
    recv = swap(partial_core.reshape(devices, ranks, cols_z, 128), both)
    recv = recv.reshape(n_sx, n_ly, ranks, cols_z, 128)
    core, second, gram = second_stage(recv, test_matrix.T, devices)
    gram = jnp.sum(swap(gram.reshape(devices, 4, 128), both), axis=0)
    gram = share(gram, both, devices).reshape(devices * 4, 128)
    q_one, sums = middle_stage(gram, second, core, devices, ranks, members)
    groups = [[b * members + m for m in range(members)] for b in range(blocks)]
    q_mine = swap(q_one, "ly", groups)
    q_mine = q_mine.reshape(rank // n_sx * (128 // members), width)
    per = sums.shape[0] // devices
    sums = swap(sums.reshape(devices, per, 8, 128), both)
    sums = jnp.sum(sums, axis=0)
    sums = share(sums, both, devices)
    sums = sums.reshape(devices * per, 8, 128)
    core_scale = math.sqrt(width / (total_x * cols_y))
    last_core, inverse = last_stage(sums, total_z, width, core_scale)
    basis = basis_stage(q_mine, inverse, math.sqrt(rank * cols_y))
    basis_second = basis.reshape(rank // n_sx, 128 // members, width)
    return (basis_t.T, basis_second, last_core)


def solution(mesh):
    return jax.shard_map(
        shards,
        mesh=mesh,
        in_specs=(P("sx", "ly", None), P(), P("ly", None), P()),
        out_specs=(P("sx", None), P("sx", "ly", None), P()),
        check_vma=False,
    )
```

```python
import functools
import math

import jax
import jax.numpy as jnp
from jax import lax
from jax.experimental import pallas as pl
from jax.experimental.pallas import tpu as pltpu
from jax.sharding import PartitionSpec as P

HI = lax.Precision.HIGHEST
F32 = jnp.float32
VMEM_LIMIT = 56 * 1024 * 1024
UNROLL = 10


GROUP = 10


def tiles_of(ref, size, row0=0):
    lanes = -(-size // 128)
    return [
        [ref[row0 + 8 * t : row0 + 8 * t + 8, 128 * l : 128 * l + 128] for l in range(lanes)]
        for t in range(size // 8)
    ]


def spread(row, tile):
    return jnp.broadcast_to(tile[row : row + 1, :], (8, 128))


def put_inverse(tiles, size, out_ref, group=GROUP):
    count = size // 8
    lanes = -(-size // 128)
    lane = lax.broadcasted_iota(jnp.int32, (8, 128), 1)
    sub = lax.broadcasted_iota(jnp.int32, (8, 128), 0)
    work = [list(r) for r in tiles]
    for g in range(0, count, group):
        end = min(g + group, count)
        done = []
        for p in range(g, end):
            l0, c0 = divmod(8 * p, 128)
            span = range(p, end)
            cols = {t: [jnp.broadcast_to(work[t][l0][:, c0 + i : c0 + i + 1], (8, 128)) for i in range(8)] for t in span}
            block = list(cols[p])
            unit = [jnp.where(sub == c, 1.0, 0.0) for c in range(8)]
            diag = None
            for i in range(8):
                diag = block[i] if i == 0 else jnp.where(sub == i, block[i], diag)
                if i == 7:
                    break
                factor = block[i] * spread(i, 1.0 / block[i])
                for m in range(i + 1, 8):
                    block[m] = block[m] - factor * spread(i, block[m])
                factor = jnp.where(sub > i, factor, 0.0)
                for c in range(i + 1):
                    unit[c] = unit[c] - factor * spread(i, unit[c])
            root = lax.rsqrt(diag)
            root = root * (1.5 - 0.5 * diag * root * root)
            inv = [u * root for u in unit]
            src = list(work[p])
            inside = (lane >= c0) & (lane < c0 + 8)
            src[l0] = jnp.where(inside, jnp.where(lane - c0 == sub, 1.0, 0.0), src[l0])
            rows = []
            for l in range(lanes):
                terms = [inv[i] * spread(i, src[l]) for i in range(8)]
                rows.append(((terms[0] + terms[1]) + (terms[2] + terms[3])) + ((terms[4] + terms[5]) + (terms[6] + terms[7])))
            for l in range(lanes):
                pos = lane + 128 * l
                out_ref[8 * p : 8 * p + 8, 128 * l : 128 * l + 128] = jnp.where(pos <= sub + 8 * p, rows[l], 0.0)
            done.append(rows)
            for t in range(p + 1, end):
                factors = []
                for m in range(8):
                    terms = [cols[t][i] * spread(m, inv[i]) for i in range(m + 1)]
                    while len(terms) > 1:
                        terms = [a + b for a, b in zip(terms[::2], terms[1::2])] + ([terms[-1]] if len(terms) % 2 else [])
                    factors.append(terms[0])
                for l in range(lanes):
                    old = work[t][l]
                    if l == l0:
                        old = jnp.where(inside, 0.0, old)
                    terms = [factors[m] * spread(m, rows[l]) for m in range(8)]
                    work[t][l] = old - (((terms[0] + terms[1]) + (terms[2] + terms[3])) + ((terms[4] + terms[5]) + (terms[6] + terms[7])))
        if end < count:
            left = jnp.concatenate([jnp.concatenate(r, axis=1) for r in done], axis=0)
            pos = lax.broadcasted_iota(jnp.int32, left.shape, 1)
            own = lax.broadcasted_iota(jnp.int32, left.shape, 0) + 8 * g
            right = jnp.where((pos > own) & (pos < 8 * end), 0.0, left)
            outer = lax.dot_general(left, right, (((0,), (0,)), ((), ())), precision=HI, preferred_element_type=F32)
            for t in range(end, count):
                for l in range(lanes):
                    pos = lane + 128 * l
                    old = work[t][l]
                    if 128 * l < 8 * end and 128 * l + 128 > 8 * g:
                        old = jnp.where((pos >= 8 * g) & (pos < 8 * end), 0.0, old)
                    work[t][l] = old - outer[8 * t : 8 * t + 8, 128 * l : 128 * l + 128]


def split(value):
    high = value.astype(jnp.bfloat16)
    rest = value - high.astype(F32)
    middle = rest.astype(jnp.bfloat16)
    low = (rest - middle.astype(F32)).astype(jnp.bfloat16)
    return high, middle, low


def dot_bf16(a, b):
    return lax.dot_general(a, b, (((1,), (0,)), ((), ())), preferred_element_type=F32)


def dot_six(a, b, transposed=False):
    rows = a.shape[0]
    dims = (((1,), (1 if transposed else 0,)), ((), ()))
    left = jnp.concatenate(split(a), axis=0)
    high, middle, low = split(b)

    def dot(x, y):
        return lax.dot_general(x, y, dims, preferred_element_type=F32)

    first = dot(left, high)
    second = dot(left[: 2 * rows], middle)
    third = dot(left[:rows], low)
    return first[:rows] + (
        (first[rows : 2 * rows] + second[:rows]) + (first[2 * rows :] + (second[rows:] + third))
    )


def first_kernel(index_ref, sketch_ref, q_ref, basis_ref, gram_ref, inv_ref, wide_ref, *, rank, scale):
    rows_x = q_ref.shape[1]
    total = wide_ref.shape[1]
    halves = rows_x // 128
    for n in range(total // 128):
        block, half = divmod(n, halves)
        rows = pl.ds(block * rank * halves + half, rank, stride=halves)
        wide_ref[:, 128 * n : 128 * n + 128] = sketch_ref[rows, :]
    gram_ref[...] = jnp.zeros_like(gram_ref)
    sketch = wide_ref[...]
    gram_ref[:, :rank] = dot_six(sketch, sketch, True)
    put_inverse(tiles_of(gram_ref, rank), rank, inv_ref)
    qt = dot_six(inv_ref[:, :rank], sketch)
    wide_ref[...] = qt
    gram_ref[:, :rank] = dot_six(qt, qt, True)
    put_inverse(tiles_of(gram_ref, rank), rank, inv_ref)
    at = pl.multiple_of(index_ref[0] * rows_x, 128)
    mine = dot_six(inv_ref[:, :rank], wide_ref[:, pl.ds(at, rows_x)])
    q_ref[...] = mine
    basis_ref[...] = scale * mine


def first_basis(sketch, index, rank, rows_x, scale):
    total = sketch.shape[0] * 128 // rank
    wide = -(-rank // 128) * 128
    shape = jax.ShapeDtypeStruct((rank, rows_x), F32)
    vmem = pl.BlockSpec(memory_space=pltpu.VMEM)
    return pl.pallas_call(
        functools.partial(first_kernel, rank=rank, scale=scale),
        out_shape=(shape, shape),
        in_specs=[pl.BlockSpec(memory_space=pltpu.SMEM), vmem],
        out_specs=(vmem, vmem),
        scratch_shapes=[
            pltpu.VMEM((rank, wide), F32),
            pltpu.VMEM((rank, wide), F32),
            pltpu.VMEM((rank, total), F32),
        ],
        compiler_params=pltpu.CompilerParams(vmem_limit_bytes=VMEM_LIMIT),
        name="first_basis",
    )(index, sketch)


def sketch_kernel(*refs):
    slab_refs, (fy_ref, fz_ref, out_ref, left_ref, sum_ref) = refs[:-5], refs[-5:]
    step = pl.program_id(0)
    rows_x, span, lanes = slab_refs[0].shape
    rank = fy_ref.shape[0]
    flat = [ref.reshape(rows_x * span, lanes) for ref in slab_refs]

    @pl.when(step == 0)
    def _():
        for n, piece in enumerate(split(fy_ref[...])):
            left_ref[n * rank : (n + 1) * rank, :] = piece

    def dot(x, y):
        dims = (((1,), (1,)), ((), ()))
        return lax.dot_general(x, y, dims, preferred_element_type=F32)

    turned = fz_ref[...].T
    total = None
    for i in range(span):
        rows = pl.ds(i, rows_x, stride=span)
        high, middle, low = split(jnp.concatenate([ref[rows, :] for ref in flat], axis=1))
        first = dot(left_ref[...], high)
        second = dot(left_ref[: 2 * rank, :], middle)
        third = dot(left_ref[:rank, :], low)
        part = first[:rank] + (
            (first[rank : 2 * rank] + second[:rank]) + (first[2 * rank :] + (second[rank:] + third))
        )
        part = part * turned[:, i : i + 1]
        total = part if total is None else total + part

    @pl.when(step == 0)
    def _():
        sum_ref[...] = total

    @pl.when(step > 0)
    def _():
        sum_ref[...] = sum_ref[...] + total

    @pl.when(step == pl.num_programs(0) - 1)
    def _():
        halves = rows_x // 128
        for n in range(halves):
            out_ref[pl.ds(n, rank, stride=halves), :] = sum_ref[:, 128 * n : 128 * n + 128]


def local_sketch(tensor, fy_t, factor_z):
    rows_x, cols_z, cols_y = tensor.shape
    rank = fy_t.shape[0]
    steps = cols_z // 8
    blocks = cols_y // 128
    return pl.pallas_call(
        sketch_kernel,
        grid=(steps,),
        out_shape=jax.ShapeDtypeStruct((rank * rows_x // 128, 128), F32),
        in_specs=[
            *(
                pl.BlockSpec((rows_x, 8, 128), functools.partial(lambda l, i: (0, i, l), l))
                for l in range(blocks)
            ),
            pl.BlockSpec((rank, cols_y), lambda i: (0, 0)),
            pl.BlockSpec((8, rank), lambda i: (i, 0)),
        ],
        out_specs=pl.BlockSpec((rank * rows_x // 128, 128), lambda i: (0, 0)),
        scratch_shapes=[
            pltpu.VMEM((3 * rank, cols_y), jnp.bfloat16),
            pltpu.VMEM((rank, rows_x), F32),
        ],
        compiler_params=pltpu.CompilerParams(vmem_limit_bytes=VMEM_LIMIT),
        name="local_sketch",
    )(*[tensor] * blocks, fy_t, factor_z)


def product_kernel(qt_ref, slab_ref, out_ref, left_ref, *, cols_z, rows_x, parts, rank_part):
    rank = parts * rank_part

    @pl.when(pl.program_id(0) == 0)
    def _():
        for n, piece in enumerate(split(qt_ref[...])):
            left_ref[n * rank : (n + 1) * rank, :] = piece

    def body(step, carry):
        z = step * 2
        left = slab_ref[pl.ds(z, rows_x, stride=cols_z), :]
        right = slab_ref[pl.ds(z + 1, rows_x, stride=cols_z), :]
        high, middle, low = split(jnp.concatenate([left, right], axis=1))
        first = dot_bf16(left_ref[...], high)
        second = dot_bf16(left_ref[: 2 * rank, :], middle)
        third = dot_bf16(left_ref[:rank, :], low)
        both = first[:rank] + (
            (first[rank : 2 * rank] + second[:rank]) + (first[2 * rank :] + (second[rank:] + third))
        )
        for s in range(parts):
            piece = both[s * rank_part : (s + 1) * rank_part]
            out_ref[s, 0, pl.ds(z, rank_part, stride=cols_z), :] = piece[:, :128]
            out_ref[s, 0, pl.ds(z + 1, rank_part, stride=cols_z), :] = piece[:, 128:]
        return carry

    lax.fori_loop(0, cols_z // 2, body, 0, unroll=UNROLL)


def product(qt, tensor, parts):
    rows_x, cols_z, cols_y = tensor.shape
    rank = qt.shape[0]
    blocks = cols_y // 128
    rank_part = rank // parts
    flat = tensor.reshape(rows_x * cols_z, cols_y)
    return pl.pallas_call(
        functools.partial(
            product_kernel, cols_z=cols_z, rows_x=rows_x, parts=parts, rank_part=rank_part
        ),
        grid=(blocks,),
        out_shape=jax.ShapeDtypeStruct((parts, blocks, rank_part * cols_z, 128), F32),
        in_specs=[
            pl.BlockSpec((rank, rows_x), lambda i: (0, 0)),
            pl.BlockSpec((rows_x * cols_z, 128), lambda i: (0, i)),
        ],
        out_specs=pl.BlockSpec((parts, 1, rank_part * cols_z, 128), lambda i: (0, i, 0, 0)),
        scratch_shapes=[pltpu.VMEM((3 * rank, rows_x), jnp.bfloat16)],
        compiler_params=pltpu.CompilerParams(vmem_limit_bytes=VMEM_LIMIT),
        name="product",
    )(qt, flat)


def second_kernel(recv_ref, test_ref, core_ref, second_ref, gram_out_ref, gram_ref, *, width):
    step = pl.program_id(0)
    core = recv_ref[0, :, 0] + recv_ref[1, :, 0]
    core = core + (recv_ref[2, :, 0] + recv_ref[3, :, 0])
    core = core.reshape(core_ref.shape)
    core_ref[...] = core
    sec = dot_six(test_ref[...], core)
    lanes = core_ref.shape[1]
    second_ref[:, pl.ds(pl.multiple_of(step * lanes, lanes), lanes)] = sec

    @pl.when(step == pl.num_programs(0) - 1)
    def _():
        whole = second_ref[...]
        gram_ref[:, :width] = dot_six(whole, whole, True)
        gram_out_ref[...] = jnp.zeros_like(gram_out_ref)
        gram_out_ref[:width, :] = gram_ref[:, :128]
        gram_out_ref[width : 2 * width, : width - 128] = gram_ref[:, 128:width]


def second_stage(recv, test_t, devices):
    parts, groups, ranks, cols_z, lanes = recv.shape
    width, total_z = test_t.shape
    gram_rows = 4 * devices
    return pl.pallas_call(
        functools.partial(second_kernel, width=width),
        grid=(ranks,),
        out_shape=(
            jax.ShapeDtypeStruct((total_z, ranks * lanes), F32),
            jax.ShapeDtypeStruct((width, ranks * lanes), F32),
            jax.ShapeDtypeStruct((gram_rows, 128), F32),
        ),
        in_specs=[
            pl.BlockSpec((parts, groups, 1, cols_z, lanes), lambda i: (0, 0, i, 0, 0)),
            pl.BlockSpec((width, total_z), lambda i: (0, 0)),
        ],
        out_specs=(
            pl.BlockSpec((total_z, lanes), lambda i: (0, i)),
            pl.BlockSpec((width, ranks * lanes), lambda i: (0, 0)),
            pl.BlockSpec((gram_rows, 128), lambda i: (0, 0)),
        ),
        scratch_shapes=[pltpu.VMEM((width, -(-width // 128) * 128), F32)],
        compiler_params=pltpu.CompilerParams(vmem_limit_bytes=VMEM_LIMIT),
        name="second_stage",
    )(recv, test_t)


def middle_kernel(gram_ref, second_ref, core_ref, q_ref, sums_ref, inv_ref, wide_ref, *, width):
    tiles = [
        [gram_ref[8 * t : 8 * t + 8, :], gram_ref[width + 8 * t : width + 8 * t + 8, :]]
        for t in range(width // 8)
    ]
    put_inverse(tiles, width, inv_ref)
    total_z = core_ref.shape[0]
    q = dot_six(inv_ref[:, :width], second_ref[...])
    members, ranks, rows, _ = q_ref.shape
    for r in range(ranks):
        turned = q[:, r * members * rows : (r + 1) * members * rows].T
        for m in range(members):
            q_ref[m, r] = turned[m * rows : (m + 1) * rows, :]
    wide_ref[:, total_z:] = jnp.zeros((width, wide_ref.shape[1] - total_z), F32)
    wide_ref[:, :total_z] = dot_six(q, core_ref[...], True)
    wide_ref[:, total_z : total_z + width] = dot_six(q, q, True)
    lanes = wide_ref.shape[1] // 128
    for t in range(width // 8):
        for l in range(lanes):
            sums_ref[t * lanes + l] = wide_ref[8 * t : 8 * t + 8, 128 * l : 128 * l + 128]
    for n in range(width // 8 * lanes, sums_ref.shape[0]):
        sums_ref[n] = jnp.zeros((8, 128), F32)


def middle_stage(gram, second, core, devices, ranks, members):
    width, pairs = second.shape
    total_z = core.shape[0]
    wide = total_z + -(-width // 128) * 128
    count = width // 8 * (wide // 128)
    count = -(-count // devices) * devices
    vmem = pl.BlockSpec(memory_space=pltpu.VMEM)
    return pl.pallas_call(
        functools.partial(middle_kernel, width=width),
        out_shape=(
            jax.ShapeDtypeStruct((members, ranks, pairs // ranks // members, width), F32),
            jax.ShapeDtypeStruct((count, 8, 128), F32),
        ),
        in_specs=[vmem, vmem, vmem],
        out_specs=(vmem, vmem),
        scratch_shapes=[
            pltpu.VMEM((width, -(-width // 128) * 128), F32),
            pltpu.VMEM((width, wide), F32),
        ],
        compiler_params=pltpu.CompilerParams(vmem_limit_bytes=VMEM_LIMIT),
        name="middle_stage",
    )(gram, second, core)


def last_kernel(sums_ref, last_ref, inv_ref, wide_ref, *, width, lanes, scale):
    first = last_ref.shape[1] // 128
    tiles = [
        [sums_ref[t * lanes + first + l] for l in range(lanes - first)] for t in range(width // 8)
    ]
    put_inverse(tiles, width, inv_ref)
    for t in range(width // 8):
        for l in range(first):
            wide_ref[8 * t : 8 * t + 8, 128 * l : 128 * l + 128] = sums_ref[t * lanes + l]
    last_ref[...] = scale * dot_six(inv_ref[:, :width], wide_ref[...])


def last_stage(sums, total_z, width, scale):
    wide = -(-width // 128) * 128
    vmem = pl.BlockSpec(memory_space=pltpu.VMEM)
    return pl.pallas_call(
        functools.partial(last_kernel, width=width, lanes=(total_z + wide) // 128, scale=scale),
        out_shape=(
            jax.ShapeDtypeStruct((width, total_z), F32),
            jax.ShapeDtypeStruct((width, wide), F32),
        ),
        in_specs=[vmem],
        out_specs=(vmem, vmem),
        scratch_shapes=[pltpu.VMEM((width, total_z), F32)],
        compiler_params=pltpu.CompilerParams(vmem_limit_bytes=VMEM_LIMIT),
        name="last_stage",
    )(sums)


def basis_kernel(q_ref, inv_ref, basis_ref, *, scale):
    basis_ref[...] = scale * dot_six(q_ref[...], inv_ref[:, : q_ref.shape[1]], True)


def basis_stage(q, inverse, scale):
    vmem = pl.BlockSpec(memory_space=pltpu.VMEM)
    return pl.pallas_call(
        functools.partial(basis_kernel, scale=scale),
        out_shape=jax.ShapeDtypeStruct(q.shape, F32),
        in_specs=[vmem, vmem],
        out_specs=vmem,
        compiler_params=pltpu.CompilerParams(vmem_limit_bytes=VMEM_LIMIT),
        name="basis_stage",
    )(q, inverse)


def swap(pieces, axes, groups=None):
    return lax.all_to_all(pieces, axes, 0, 0, axis_index_groups=groups, tiled=True)


def share(piece, axes, count):
    return swap(jnp.broadcast_to(piece[None], (count,) + piece.shape), axes)


def shards(tensor, factor_y, factor_z, test_matrix):
    rows_x, cols_z, cols_y = tensor.shape
    rank = factor_y.shape[1]
    width = test_matrix.shape[1]
    n_sx = lax.axis_size("sx")
    n_ly = lax.axis_size("ly")
    both = ("sx", "ly")
    devices = n_sx * n_ly
    total_x = rows_x * n_sx
    total_z = cols_z * n_ly
    halves = rows_x // 128
    local = local_sketch(tensor, factor_y.T, factor_z)
    local = swap(local.reshape(rank, halves, 128), "ly")
    mine = jnp.sum(local.reshape(n_ly, rank // n_ly, halves, 128), axis=0)
    sketch = share(mine, both, devices).reshape(n_sx * rank * halves, 128)
    index = lax.axis_index("sx").astype(jnp.int32).reshape(1)
    qt, basis_t = first_basis(sketch, index, rank, rows_x, math.sqrt(total_x))

    blocks = cols_y // 128
    members = n_ly // blocks
    ranks = rank // (n_sx * members)
    partial_core = product(qt, tensor, n_sx)
    recv = swap(partial_core.reshape(devices, ranks, cols_z, 128), both)
    recv = recv.reshape(n_sx, n_ly, ranks, cols_z, 128)
    core, second, gram = second_stage(recv, test_matrix.T, devices)
    gram = jnp.sum(swap(gram.reshape(devices, 4, 128), both), axis=0)
    gram = share(gram, both, devices).reshape(devices * 4, 128)
    q_one, sums = middle_stage(gram, second, core, devices, ranks, members)
    groups = [[b * members + m for m in range(members)] for b in range(blocks)]
    q_mine = swap(q_one, "ly", groups)
    q_mine = q_mine.reshape(rank // n_sx * (128 // members), width)
    per = sums.shape[0] // devices
    sums = swap(sums.reshape(devices, per, 8, 128), both)
    sums = jnp.sum(sums, axis=0)
    sums = share(sums, both, devices)
    sums = sums.reshape(devices * per, 8, 128)
    core_scale = math.sqrt(width / (total_x * cols_y))
    last_core, inverse = last_stage(sums, total_z, width, core_scale)
    basis = basis_stage(q_mine, inverse, math.sqrt(rank * cols_y))
    basis_second = basis.reshape(rank // n_sx, 128 // members, width)
    return (basis_t.T, basis_second, last_core)


def solution(mesh):
    return jax.shard_map(
        shards,
        mesh=mesh,
        in_specs=(P("sx", "ly", None), P(), P("ly", None), P()),
        out_specs=(P("sx", None), P("sx", "ly", None), P()),
        check_vma=False,
    )
```
